128 devices in a mesh: seq: 16 (over x, z), head: 8 (over y, core).
Axes of the slice: x: 4, y: 4, z: 4, core: 2. Of those that a mesh axis runs over, the one named last changes fastest.
Arguments:
- tokens: bfloat16 [32768, 2048], P('seq'), may hold values from -6 to 6
- norm_gain: float32 [2048], replicated, may hold values from 0.1 to 1.9
- query_weight: bfloat16 [2048, 2048], P(None, 'head'), may hold values from -0.125 to 0.125
- key_weight: bfloat16 [2048, 2048], P(None, 'head'), may hold values from -1 to 1
- value_weight: bfloat16 [2048, 2048], P(None, 'head'), may hold values from -0.125 to 0.125
- beta_weight: bfloat16 [2048, 16], P(None, 'head'), may hold values from -1 to 1
- out_gain: float32 [128], replicated, may hold values from 0.1 to 1.9
- output_weight: bfloat16 [2048, 2048], P('head'), may hold values from -0.1875 to 0.1875
- block_doc: int32 [512], P('seq'), may hold values from 0 to 3, never falling along the last dimension, each value on 1 to 192 neighbouring positions
Outputs:
- mixed: bfloat16 [32768, 2048], P('seq', 'head')
The draws below stay inside these ranges and needn't reach their ends.
Inputs may be any that keep to these rules, and one draw needn't show every extreme that they name: `block_doc`: document numbers never fall along the window; each document covers 1 to 192 whole blocks, and one covers exactly that many.
All inputs are finite; a program needn't handle non-finite values.
Results may differ from the reference program's by a relative error of at most 0.02.
Values may be sent and summed in bfloat16 or wider, within the bound.
A program may use at most 128 MiB of HBM per device.

```python
import math
import jax
import jax.numpy as jnp
import numpy as np
from jax import lax

D = 2048
H = 16
DK = 128
BLOCK = 64
TOK_DEV = 2048
TOKENS = 32768
BLOCKS = 512
N_SEQ = 16


def shared_parts(key):
    base = jax.random.fold_in(key, 7001)
    common = jnp.clip(jax.random.normal(jax.random.fold_in(base, 1), (D,), jnp.float32), -3.0, 3.0)
    direction = jnp.clip(jax.random.normal(jax.random.fold_in(base, 2), (H * DK,), jnp.float32), -3.0, 3.0)
    return (common, direction)


def draw_tokens(key, part):
    common, direction = shared_parts(key)
    noise_key = jax.random.fold_in(key, 11)
    noise_part = jnp.clip(jax.random.normal(noise_key, (TOKENS, D), jnp.float32), -3.0, 3.0)
    combined = 0.5 * common[None, :] + noise_part
    return combined.astype(jnp.bfloat16)


def draw_key_weight(key, part):
    common, direction = shared_parts(key)
    noise_key = jax.random.fold_in(key, 21)
    random_part = jnp.clip(jax.random.normal(noise_key, (D, H * DK), jnp.float32), -4.0, 4.0)
    combined = random_part * D ** (-0.5) + 6.0 * common[:, None] * direction[None, :] / D
    return jnp.clip(combined, -1.0, 1.0).astype(jnp.bfloat16)


def draw_beta_weight(key, part):
    common, direction = shared_parts(key)
    noise_key = jax.random.fold_in(key, 31)
    random_part = jnp.clip(jax.random.normal(noise_key, (D, H), jnp.float32), -4.0, 4.0)
    strength = jax.random.uniform(jax.random.fold_in(key, 32), (H,), jnp.float32, -9.0, 9.0)
    combined = 0.3 * random_part * D ** (-0.5) + common[:, None] * strength[None, :] / D
    return jnp.clip(combined, -1.0, 1.0).astype(jnp.bfloat16)


def raised(values, rng, source, target, parts, factor):
    def block_of(position):
        return (jnp.arange(values.shape[position]) // (values.shape[position] // parts)).reshape((-1,) + (1,) * (values.ndim - 1 - position))

    first = jax.random.permutation(rng, parts)[block_of(target)]
    second = (block_of(target) + parts // 2) % parts
    return jnp.where((block_of(source) == first) | (block_of(source) == second), factor * values, values)


def block_levels(own_key, dims, shards, least, largest):
    def one(axis_at, parts):
        steps = jax.random.uniform(jax.random.fold_in(jax.random.fold_in(own_key, 6), axis_at), (parts,), jnp.float32, least / len(shards), largest / len(shards))
        return jnp.repeat(jnp.exp(steps), dims[axis_at] // parts).reshape((-1,) + (1,) * (len(dims) - axis_at - 1))

    loudness = one(*shards[0])
    for cut in shards[1:]:
        loudness = loudness * one(*cut)
    return loudness


def length_profile(amount, total, bound, lean):
    weights = [(1 << 20) // math.isqrt(rank ** lean) + 1 for rank in range(2, amount + 1)]
    rest, given = total - bound - (amount - 1), [1] * (amount - 1)
    while rest > 0:
        free = [i for i in range(amount - 1) if given[i] < bound]
        whole, left = sum([weights[i] for i in free]), rest
        for i in free:
            more = min(bound - given[i], max(1, left * weights[i] // whole), rest)
            given[i] = given[i] + more
            rest = rest - more
    return np.array([bound] + given)


def uneven_parts(stream_key, amount, total, most, skew):
    if amount == 2:
        one = jax.random.randint(stream_key, (), max(1, total - most), min(most, total - 1) + 1)
        return jnp.stack([one, total - one])
    tallies = jnp.asarray(length_profile(amount, total, most, skew), jnp.int32)
    pairs = (amount - 1) // 2
    source_of, taker = tallies[1:1 + 2 * pairs:2], tallies[2:2 + 2 * pairs:2]
    slack = jnp.minimum(source_of - 1, most - taker)
    shifted = jax.random.randint(jax.random.fold_in(stream_key, 1), (pairs,), 0, 1 << 20) % (slack + 1)
    tallies = tallies.at[1:1 + 2 * pairs:2].set(source_of - shifted).at[2:2 + 2 * pairs:2].set(taker + shifted)
    return tallies[jax.random.permutation(jax.random.fold_in(stream_key, 2), amount)]


def centred(rng, shape, spread, most, shards=(), held_as=jnp.bfloat16):
    gain = block_levels(rng, shape, shards, -0.22, 0.18) if shards else 1.0
    result = jax.random.normal(rng, shape, jnp.float32) * spread * gain
    return jnp.minimum(jnp.maximum(result, -most), most).astype(held_as)


def noise_with(stream_key, extent, scale, limit, pieces, heavy, kind=jnp.bfloat16):
    result = scale * jax.random.normal(stream_key, extent, jnp.float32)
    if pieces:
        result = result * block_levels(stream_key, extent, pieces, -0.22, 0.18)
    return jnp.clip(raised(result, jax.random.fold_in(stream_key, 3), *heavy), -limit, limit).astype(kind)


def setup_inputs(seed: int = 0) -> dict:
    streams_of = jax.random.split(jax.random.key(seed), 10)
    return {
        "tokens": draw_tokens(jax.random.fold_in(streams_of[9], 71), 0),
        "norm_gain": jnp.clip(1.0 + 0.18 * jax.random.normal(streams_of[1], (D,), jnp.float32), 0.1, 1.9),
        "query_weight": centred(streams_of[2], (D, H * DK), D ** -0.5, 0.125, ((1, 8),)),
        "key_weight": draw_key_weight(jax.random.fold_in(streams_of[9], 71), 0),
        "value_weight": centred(streams_of[4], (D, H * DK), D ** -0.5, 0.125, ((1, 8),)),
        "beta_weight": draw_beta_weight(jax.random.fold_in(streams_of[9], 71), 0),
        "out_gain": jnp.clip(1.0 + 0.18 * jax.random.normal(streams_of[6], (DK,), jnp.float32), 0.1, 1.9),
        "output_weight": noise_with(streams_of[7], (H * DK, D), (H * DK) ** -0.5, 0.1875, ((0, 8),), (0, 1, 8, 2.0)),
        "block_doc": jnp.searchsorted(jnp.cumsum(uneven_parts(streams_of[8], N_SEQ // 4, BLOCKS, 6 * TOK_DEV // BLOCK, 0)), jnp.arange(BLOCKS), side="right").astype(jnp.int32),
    }


norm_eps = 1e-05
key_eps = 1e-06

def block_parts(block_q, block_k, block_v, block_b):
    highest = lax.Precision.HIGHEST
    size = block_k.shape[1]
    positions = jnp.arange(size)
    below = positions[:, None] > positions[None, :]
    causal = positions[:, None] >= positions[None, :]
    key_gram = jnp.einsum('hcd,hed->hce', block_k, block_k, precision=highest)
    unit_lower = jnp.where(below, block_b[:, :, None] * key_gram, 0.0) + jnp.eye(size, dtype=block_k.dtype)
    right_side = jnp.concatenate([block_b[:, :, None] * block_k, block_b[:, :, None] * block_v], axis=2)
    solved = lax.linalg.triangular_solve(unit_lower, right_side, left_side=True, lower=True)
    width = block_k.shape[2]
    scores = jnp.where(causal, jnp.einsum('hcd,hed->hce', block_q, block_k, precision=highest), 0.0)
    return (solved[:, :, :width], solved[:, :, width:], scores)

def unit_norm(values):
    return values / jnp.sqrt(lax.optimization_barrier(jnp.sum(values * values, axis=-1, keepdims=True)) + key_eps)

def reference(tokens, norm_gain, query_weight, key_weight, value_weight, beta_weight, out_gain, output_weight, block_doc):
    highest = lax.Precision.HIGHEST
    length = tokens.shape[0]
    floats = tokens.astype(jnp.float32)
    normed = (floats / jnp.sqrt(lax.optimization_barrier(jnp.mean(floats * floats, axis=1, keepdims=True)) + norm_eps) * norm_gain).astype(jnp.bfloat16)
    queries = unit_norm(jax.nn.silu(jnp.dot(normed.astype(jnp.float32), query_weight.astype(jnp.float32), preferred_element_type=jnp.float32)).reshape(length, H, DK))
    keys = unit_norm(jax.nn.silu(jnp.dot(normed.astype(jnp.float32), key_weight.astype(jnp.float32), preferred_element_type=jnp.float32)).reshape(length, H, DK))
    values = jnp.dot(normed.astype(jnp.float32), value_weight.astype(jnp.float32), preferred_element_type=jnp.float32).reshape(length, H, DK)
    beta = jax.nn.sigmoid(jnp.dot(normed.astype(jnp.float32), beta_weight.astype(jnp.float32), preferred_element_type=jnp.float32))
    count = length // BLOCK

    def blocked(array):
        return array.reshape(count, BLOCK, H, DK).transpose(0, 2, 1, 3)

    def advance(carry, inputs):
        state, previous = carry
        block_q, block_k, block_v, block_b, doc_id = inputs
        state = jnp.where(doc_id != previous, jnp.zeros_like(state), state)
        w_keys, u_values, scores = block_parts(block_q, block_k, block_v, block_b)
        fresh = u_values - jnp.einsum('hcd,hde->hce', w_keys, state, precision=highest)
        output = jnp.einsum('hcd,hde->hce', block_q, state, precision=highest) + jnp.einsum('hce,hef->hcf', scores, fresh, precision=highest)
        state = state + jnp.einsum('hcd,hce->hde', block_k, fresh, precision=highest)
        return ((state, doc_id), output)
    start = (jnp.zeros((H, DK, DK), jnp.float32), block_doc[0])
    inputs = (blocked(queries), blocked(keys), blocked(values), beta.reshape(count, BLOCK, H).transpose(0, 2, 1), block_doc)
    carry_end, outputs = lax.scan(advance, start, inputs)
    heads_out = outputs.transpose(0, 2, 1, 3).reshape(length, H, DK)
    normed_out = heads_out / jnp.sqrt(lax.optimization_barrier(jnp.mean(heads_out * heads_out, axis=2, keepdims=True)) + norm_eps) * out_gain
    normed_out = normed_out.reshape(length, H * DK).astype(jnp.bfloat16)
    return jnp.dot(normed_out.astype(jnp.float32), output_weight.astype(jnp.float32), preferred_element_type=jnp.float32).astype(jnp.bfloat16)
```

```python
import jax
import jax.numpy as jnp
from jax import lax
from jax.experimental import pallas as pl
from jax.experimental.pallas import tpu as pltpu
from jax.sharding import PartitionSpec as P

norm_eps = 1e-05
key_eps = 1e-06
BLOCK = 64
MOST_BLOCKS = 192
DK = 128
STEP = 256
f32 = jnp.float32
bf16 = jnp.bfloat16
LEVELS = (2, 4, 8, 16, 32, 64)


def dot(a, b):
    return jnp.dot(a, b, preferred_element_type=f32)


def dot_nt(a, b):
    return lax.dot_general(a, b, (((1,), (1,)), ((), ())), preferred_element_type=f32)


def dot_tn(a, b):
    return lax.dot_general(a, b, (((0,), (0,)), ((), ())), preferred_element_type=f32)


def unit(values):
    act = values * jax.nn.sigmoid(values)
    return act * lax.rsqrt(jnp.sum(act * act, axis=1, keepdims=True) + key_eps)


def fill_masks(strict, causal, pair, off):
    shape = (STEP, STEP)
    row = lax.broadcasted_iota(jnp.int32, shape, 0)
    col = lax.broadcasted_iota(jnp.int32, shape, 1)
    same = (row // DK) == (col // DK)
    strict[...] = jnp.where(same & (row > col), 1.0, 0.0).astype(f32)
    causal[...] = jnp.where(same & (row >= col), 1.0, 0.0).astype(f32)
    pair[...] = jnp.where((row // 2 == col // 2) & (row > col), 1.0, 0.0).astype(f32)
    for n, s in enumerate(LEVELS):
        hit = (row // (2 * s) == col // (2 * s)) & (row // s > col // s)
        off[n] = jnp.where(hit, 1.0, 0.0).astype(bf16)


def delta_step(kf, vf, qb, beta, doc, i, ps, masks):
    strict, causal, pair, off = masks
    d = [doc[4 * i + j] for j in range(4)]
    before = doc[jnp.maximum(4 * i - 1, 0)]
    link = [
        jnp.where((before == d[0]) | (i == 0), 1.0, 0.0).astype(f32),
        jnp.where(d[1] == d[2], 1.0, 0.0).astype(f32),
    ]
    join = [
        jnp.where(d[0] == d[1], 1.0, 0.0).astype(f32),
        jnp.where(d[2] == d[3], 1.0, 0.0).astype(f32),
    ]
    row = lax.broadcasted_iota(jnp.int32, (STEP, 1), 0)
    second = (row % DK) >= BLOCK
    chunk1 = row >= DK
    join_r = jnp.where(chunk1, join[1], join[0])
    link_r = jnp.where(chunk1, link[1], link[0])
    enters = jnp.where(second, link_r * join_r, link_r)
    leaves = jnp.where(second, 1.0, join_r)
    col = lax.broadcasted_iota(jnp.int32, (1, STEP), 1)
    cross = jnp.where(second, join_r, 1.0)
    col_first = (col % DK) < BLOCK
    kb = kf.astype(bf16)
    doc_mask = jnp.where(col_first, cross, 1.0)
    a = dot_nt(kb, kb) * beta * (strict[...] * doc_mask)
    scores = dot_nt(qb, kb) * (causal[...] * doc_mask)
    a_hi = a.astype(bf16)
    a_lo = (a - a_hi.astype(f32)).astype(bf16)
    eye = causal[...] - strict[...]
    x = eye - a * pair[...]
    for n in range(len(LEVELS)):
        xb = x.astype(bf16)
        x = x - dot(xb, dot(a_hi * off[n], xb).astype(bf16))
    xb = x.astype(bf16)
    kr = kb.astype(f32)
    right = jnp.concatenate([beta * enters * kr, beta * vf], axis=1)
    y = dot(xb, right.astype(bf16)).astype(bf16)
    left = right - y.astype(f32) - dot(a_hi, y) - dot(a_lo, y)
    wu = (y.astype(f32) + dot(xb, left.astype(bf16))).astype(bf16)
    mixed = dot(scores.astype(bf16), wu)
    reach = (enters * qb.astype(f32) - mixed[:, :DK]).astype(bf16)
    k_end = (kr * leaves).astype(bf16)
    outs, carried = [], []
    for c in range(2):
        rows = slice(c * DK, (c + 1) * DK)
        step = dot_tn(k_end[rows], wu[rows])
        state = ps[...]
        sb = state.astype(bf16)
        seen = dot(reach[rows], sb)
        carried.append(seen[:, :DK])
        outs.append(mixed[rows, DK:] + seen[:, DK:])
        moved = dot(step[:, :DK].astype(bf16), sb)
        keep = link[c] * join[c]
        gain = jnp.concatenate([jnp.zeros((DK, DK), f32), step[:, DK:]], axis=1)
        ps[...] = keep * state - moved + gain
    return jnp.concatenate(outs, axis=0), jnp.concatenate(carried, axis=0)


def local_kernel(
    doc, tok, gain, wq, wk, wv, wb, out, carried, ps_out,
    weights, normed, later_q, beta_all, ps, strict, causal, pair, off, sems,
):
    h, i = pl.program_id(0), pl.program_id(1)
    rows = pl.ds(pl.multiple_of(i * STEP, STEP), STEP)
    masks = (strict, causal, pair, off)

    @pl.when((h == 0) & (i == 0))
    def _():
        copies = []
        for n, (source, column) in enumerate(
            [(wk, 0), (wv, 0), (wk, 1), (wv, 1), (wq, 0), (wq, 1)]
        ):
            copies.append(
                pltpu.make_async_copy(
                    source.at[:, column * DK : (column + 1) * DK],
                    weights.at[:, n * DK : (n + 1) * DK],
                    sems.at[n],
                )
            )
        for copy in copies:
            copy.start()
        fill_masks(*masks)
        weights[:, 6 * DK :] = jnp.concatenate(
            [wb[...], jnp.zeros((wb.shape[0], DK - wb.shape[1]), bf16)], axis=1
        )
        for copy in copies:
            copy.wait()

    @pl.when(i == 0)
    def _():
        row = lax.broadcasted_iota(jnp.int32, (DK, 2 * DK), 0)
        col = lax.broadcasted_iota(jnp.int32, (DK, 2 * DK), 1)
        ps[...] = jnp.where(row == col, 1.0, 0.0).astype(f32)

    @pl.when(h == 0)
    def _():
        floats = tok[...].astype(f32)
        scale = lax.rsqrt(jnp.mean(floats * floats, axis=1, keepdims=True) + norm_eps)
        n = (floats * scale * gain[...]).astype(bf16)
        normed[rows, :] = n
        rest = dot(n, weights[:, 4 * DK :])
        q0 = unit(rest[:, :DK]).astype(bf16)
        later_q[0, rows, :] = q0
        later_q[1, rows, :] = unit(rest[:, DK : 2 * DK]).astype(bf16)
        beta_all[rows, :] = jax.nn.sigmoid(rest[:, 2 * DK :])

    kv = dot(normed[rows, :], weights[:, pl.ds(pl.multiple_of(h * 2 * DK, 2 * DK), 2 * DK)])
    kf = unit(kv[:, :DK])
    both = beta_all[rows, :]
    beta = jnp.where(h == 0, both[:, 0:1], both[:, 1:2])
    o, c = delta_step(kf, kv[:, DK:], later_q[h, rows, :], beta, doc, i, ps, masks)
    out[0] = o
    carried[0] = c.astype(bf16)

    @pl.when(i == pl.num_programs(1) - 1)
    def _():
        ps_out[0] = ps[...]


def local_pass(doc, tokens, gain, wq, wk, wv, wb):
    length, width = tokens.shape
    heads = wb.shape[1]
    steps = length // STEP
    any_spec = pl.BlockSpec(memory_space=pl.ANY)
    return pl.pallas_call(
        local_kernel,
        grid_spec=pltpu.PrefetchScalarGridSpec(
            num_scalar_prefetch=1,
            grid=(heads, steps),
            in_specs=[
                pl.BlockSpec((STEP, width), lambda h, i, doc: (jnp.where(h == 0, i, steps - 1), 0)),
                pl.BlockSpec((1, width), lambda h, i, doc: (0, 0)),
                any_spec,
                any_spec,
                any_spec,
                pl.BlockSpec(wb.shape, lambda h, i, doc: (0, 0)),
            ],
            out_specs=[
                pl.BlockSpec((1, STEP, DK), lambda h, i, doc: (h, i, 0)),
                pl.BlockSpec((1, STEP, DK), lambda h, i, doc: (h, i, 0)),
                pl.BlockSpec((1, DK, 2 * DK), lambda h, i, doc: (h, 0, 0)),
            ],
            scratch_shapes=[
                pltpu.VMEM((width, 7 * DK), bf16),
                pltpu.VMEM((length, width), bf16),
                pltpu.VMEM((heads, length, DK), bf16),
                pltpu.VMEM((length, DK), f32),
                pltpu.VMEM((DK, 2 * DK), f32),
                pltpu.VMEM((STEP, STEP), f32),
                pltpu.VMEM((STEP, STEP), f32),
                pltpu.VMEM((STEP, STEP), f32),
                pltpu.VMEM((len(LEVELS), STEP, STEP), bf16),
                pltpu.SemaphoreType.DMA((6,)),
            ],
        ),
        out_shape=[
            jax.ShapeDtypeStruct((heads, length, DK), f32),
            jax.ShapeDtypeStruct((heads, length, DK), bf16),
            jax.ShapeDtypeStruct((heads, DK, 2 * DK), f32),
        ],
        compiler_params=pltpu.CompilerParams(vmem_limit_bytes=48 << 20),
        name="local_pass",
    )(doc, tokens, gain, wq, wk, wv, wb)


def output_kernel(out, carried, incoming, gain, weight, partial):
    columns = []
    for h in range(out.shape[0]):
        o = out[h] + dot(carried[h], incoming[h])
        scale = lax.rsqrt(jnp.mean(o * o, axis=1, keepdims=True) + norm_eps)
        columns.append((o * scale * gain[...]).astype(bf16))
    partial[...] = dot(jnp.concatenate(columns, axis=1), weight[...]).astype(bf16)


def output_pass(out, carried, incoming, gain, weight):
    heads, length, _ = out.shape
    return pl.pallas_call(
        output_kernel,
        grid=(length // STEP,),
        in_specs=[
            pl.BlockSpec((heads, STEP, DK), lambda i: (0, i, 0)),
            pl.BlockSpec((heads, STEP, DK), lambda i: (0, i, 0)),
            pl.BlockSpec(incoming.shape, lambda i: (0, 0, 0)),
            pl.BlockSpec((1, DK), lambda i: (0, 0)),
            pl.BlockSpec(weight.shape, lambda i: (0, 0)),
        ],
        out_specs=pl.BlockSpec((STEP, weight.shape[1]), lambda i: (i, 0)),
        out_shape=jax.ShapeDtypeStruct((length, weight.shape[1]), bf16),
        compiler_params=pltpu.CompilerParams(vmem_limit_bytes=32 << 20),
        name="output_pass",
    )(out, carried, incoming, gain, weight)


def passed_along(block, axis):
    route = [(i, i + 1) for i in range(lax.axis_size(axis) - 1)]
    return lax.ppermute(block, axis, route)


def local(tokens, norm_gain, wq, wk, wv, wb, out_gain, wo, block_doc):
    count = block_doc.shape[0]
    out, carried, ps = local_pass(block_doc, tokens, norm_gain[None, :], wq, wk, wv, wb)
    transit, state = ps[:, :, :DK], ps[:, :, DK:]
    first = block_doc[0:1].astype(f32)
    last = block_doc[count - 1 : count].astype(bf16)
    before = passed_along(last, "seq").astype(f32)
    follows = (before[0] == first[0]) & (lax.axis_index("seq") > 0)
    incoming = jnp.zeros_like(state)
    for turn in range(MOST_BLOCKS // count):
        end = state if turn == 0 else jnp.einsum("hde,hef->hdf", transit, incoming) + state
        got = passed_along(end.astype(bf16), "seq").astype(f32)
        incoming = jnp.where(follows, got, 0.0)
    partial = output_pass(out, carried, incoming.astype(bf16), out_gain[None, :], wo)
    return lax.psum_scatter(partial, "head", scatter_dimension=1, tiled=True)


def solution(mesh):
    in_specs = (
        P("seq", None),
        P(),
        P(None, "head"),
        P(None, "head"),
        P(None, "head"),
        P(None, "head"),
        P(),
        P("head", None),
        P("seq"),
    )
    return jax.shard_map(
        local, mesh=mesh, in_specs=in_specs, out_specs=P("seq", "head"), check_vma=False
    )
```

```python
import jax
import jax.numpy as jnp
from jax import lax
from jax.experimental import pallas as pl
from jax.experimental.pallas import tpu as pltpu
from jax.sharding import PartitionSpec as P

norm_eps = 1e-05
key_eps = 1e-06
BLOCK = 64
MOST_BLOCKS = 192
DK = 128
STEP = 256
TILE = 512
f32 = jnp.float32
bf16 = jnp.bfloat16
LEVELS = (2, 4, 8, 16, 32, 64)


def dot(a, b):
    return jnp.dot(a, b, preferred_element_type=f32)


def dot_nt(a, b):
    return lax.dot_general(a, b, (((1,), (1,)), ((), ())), preferred_element_type=f32)


def dot_tn(a, b):
    return lax.dot_general(a, b, (((0,), (0,)), ((), ())), preferred_element_type=f32)


def unit(values):
    act = values * jax.nn.sigmoid(values)
    return act * lax.rsqrt(jnp.sum(act * act, axis=1, keepdims=True) + key_eps)


def fill_masks(strict, causal, pair, off):
    shape = (STEP, STEP)
    row = lax.broadcasted_iota(jnp.int32, shape, 0)
    col = lax.broadcasted_iota(jnp.int32, shape, 1)
    same = (row // DK) == (col // DK)
    strict[...] = jnp.where(same & (row > col), 1.0, 0.0).astype(f32)
    if causal is not None:
        causal[...] = jnp.where(same & (row >= col), 1.0, 0.0).astype(f32)
    pair[0] = jnp.where((row // 2 == col // 2) & (row > col), 1.0, 0.0).astype(bf16)
    pair[1] = jnp.where(row == col, 1.0, 0.0).astype(bf16)
    for n, s in enumerate(LEVELS):
        hit = (row // (2 * s) == col // (2 * s)) & (row // s > col // s)
        off[n] = jnp.where(hit, 1.0, 0.0).astype(bf16)


def scaled_weight(weight, gain):
    column = jnp.transpose(jnp.broadcast_to(gain[...], (DK, gain.shape[1])))
    parts = [
        weight[:, n * DK : (n + 1) * DK].astype(f32) * column for n in range(weight.shape[1] // DK)
    ]
    return jnp.concatenate(parts, axis=1).astype(bf16)


def doc_masks(doc, at):
    d = [doc[at + j] for j in range(4)]
    before = doc[jnp.maximum(at - 1, 0)]
    link = [
        jnp.where((before == d[0]) | (at == 0), 1.0, 0.0).astype(f32),
        jnp.where(d[1] == d[2], 1.0, 0.0).astype(f32),
    ]
    join = [
        jnp.where(d[0] == d[1], 1.0, 0.0).astype(f32),
        jnp.where(d[2] == d[3], 1.0, 0.0).astype(f32),
    ]
    row = lax.broadcasted_iota(jnp.int32, (STEP, 1), 0)
    second = (row % DK) >= BLOCK
    join_r = jnp.where(row >= DK, join[1], join[0])
    link_r = jnp.where(row >= DK, link[1], link[0])
    enters = jnp.where(second, link_r * join_r, link_r)
    leaves = jnp.where(second, 1.0, join_r)
    cross = jnp.where(second, join_r, 1.0)
    col = lax.broadcasted_iota(jnp.int32, (1, STEP), 1)
    full = jnp.where((col % DK) < BLOCK, cross, 1.0)
    return enters, leaves, full, [link[c] * join[c] for c in range(2)]


def interleave(main, side, every):
    count = 0
    for _ in main:
        count += 1
        if count % every == 0:
            next(side, None)
    for _ in side:
        pass


def project_keys(x, scale_out, weights, kbuf, vbuf, bbuf, slot):
    halves = x.shape[0] // STEP
    scales = []
    for m in range(halves):
        rows = slice(m * STEP, (m + 1) * STEP)
        floats = x[rows, :].astype(f32)
        r = lax.rsqrt(jnp.mean(floats * floats, axis=1, keepdims=True) + norm_eps)
        scales.append(r)
        scale_out[rows, :] = jnp.broadcast_to(r, (STEP, DK))
        yield
        b = dot(x[rows, :], weights[:, 4 * DK :]) * r
        bbuf[slot, rows, :] = jax.nn.sigmoid(b)
        yield
        for h in range(2):
            kv = dot(x[rows, :], weights[:, 2 * h * DK : 2 * (h + 1) * DK]) * r
            kbuf[slot, h, rows, :] = unit(kv[:, :DK]).astype(bf16)
            vbuf[slot, h, rows, :] = kv[:, DK:]
            yield


def solve_keys(doc, at, kbuf, vbuf, bbuf, slot, ps, masks, wu_out, ps_all):
    strict, pair, off, wu_buf, end_buf = masks
    halves = kbuf.shape[2] // STEP
    groups = [(h, g) for g in range(halves) for h in range(2)]
    dm = [doc_masks(doc, at + 4 * g) for g in range(halves)]
    keys, a_hi, a_lo, xb, t, right, y, wu = {}, {}, {}, {}, {}, {}, {}, {}
    beta = {}
    for h, g in groups:
        rows = slice(g * STEP, (g + 1) * STEP)
        keys[h, g] = kbuf[slot, h, rows, :]
        beta[h, g] = bbuf[slot, rows, h : h + 1]
        a = dot_nt(keys[h, g], keys[h, g]) * beta[h, g] * (strict[...] * dm[g][2])
        hi = a.astype(bf16)
        a_hi[h, g] = hi
        a_lo[h, g] = (a - hi.astype(f32)).astype(bf16)
        xb[h, g] = pair[1] - hi * pair[0]
        yield
    for n in range(len(LEVELS)):
        for at_group in groups:
            t[at_group] = dot(a_hi[at_group] * off[n], xb[at_group]).astype(bf16)
        yield
        for at_group in groups:
            xb[at_group] = xb[at_group] - dot(xb[at_group], t[at_group]).astype(bf16)
        yield
    for h, g in groups:
        rows = slice(g * STEP, (g + 1) * STEP)
        b = beta[h, g]
        right[h, g] = jnp.concatenate(
            [(b * dm[g][0]) * keys[h, g].astype(f32), b * vbuf[slot, h, rows, :]], axis=1
        )
        y[h, g] = dot(xb[h, g], right[h, g].astype(bf16)).astype(bf16)
    yield
    left = {}
    for k in groups:
        rest = right[k] - y[k].astype(f32) - dot(a_hi[k], y[k]) - dot(a_lo[k], y[k])
        left[k] = rest.astype(bf16)
    yield
    for h, g in groups:
        wu[h, g] = (y[h, g].astype(f32) + dot(xb[h, g], left[h, g])).astype(bf16)
        wu_out[h, g * STEP : (g + 1) * STEP, :] = wu[h, g]
    yield
    step = {}
    for h, g in groups:
        k_end = (keys[h, g].astype(f32) * dm[g][1]).astype(bf16)
        for c in range(2):
            rows = slice(c * DK, (c + 1) * DK)
            step[h, g, c] = dot_tn(k_end[rows], wu[h, g][rows])
    yield
    for g in range(halves):
        for c in range(2):
            for h in range(2):
                state = ps[h]
                sb = state.astype(bf16)
                ps_all[h, 2 * g + c] = sb
                move = step[h, g, c]
                moved = dot(move[:, :DK].astype(bf16), sb)
                gain = jnp.concatenate([jnp.zeros((DK, DK), f32), move[:, DK:]], axis=1)
                ps[h] = dm[g][3][c] * state - moved + gain
            yield


def keys_kernel(
    doc, x, gain, wk, wv, wb, k_out, wu_out, ps_all, ps_end, scale_out,
    weights, kbuf, vbuf, bbuf, ps, strict, pair, off,
):
    i, last = pl.program_id(0), pl.num_programs(0) - 1
    tile = x.shape[0]
    blocks = tile // BLOCK

    def project():
        return project_keys(x, scale_out, weights, kbuf, vbuf, bbuf, i % 2)

    def solve():
        slot = (i + 1) % 2
        k_out[...] = kbuf[slot]
        return solve_keys(
            doc, (i - 1) * blocks, kbuf, vbuf, bbuf, slot, ps,
            (strict, pair, off, None, None), wu_out, ps_all,
        )

    @pl.when(i == 0)
    def _():
        fill_masks(strict, None, pair, off)
        sk, sv = scaled_weight(wk, gain), scaled_weight(wv, gain)
        for h in range(2):
            weights[:, 2 * h * DK : (2 * h + 1) * DK] = sk[:, h * DK : (h + 1) * DK]
            weights[:, (2 * h + 1) * DK : (2 * h + 2) * DK] = sv[:, h * DK : (h + 1) * DK]
        wide = jnp.concatenate(
            [wb[...], jnp.zeros((wb.shape[0], DK - wb.shape[1]), bf16)], axis=1
        )
        weights[:, 4 * DK :] = scaled_weight(wide, gain)
        row = lax.broadcasted_iota(jnp.int32, (DK, 2 * DK), 0)
        col = lax.broadcasted_iota(jnp.int32, (DK, 2 * DK), 1)
        for h in range(2):
            ps[h] = jnp.where(row == col, 1.0, 0.0).astype(f32)
        for _ in project():
            pass

    @pl.when((i > 0) & (i < last))
    def _():
        interleave(solve(), project(), 2)

    @pl.when(i == last)
    def _():
        for _ in solve():
            pass
        for h in range(2):
            ps_end[h] = ps[h].astype(bf16)


def keys_pass(doc, tokens, gain, wk, wv, wb):
    length, width = tokens.shape
    heads = wb.shape[1]
    steps = length // TILE
    chunks = TILE // DK
    after = lambda i: jnp.maximum(i - 1, 0)
    whole = lambda shape: pl.BlockSpec(shape, lambda i, doc: (0,) * len(shape))
    return pl.pallas_call(
        keys_kernel,
        grid_spec=pltpu.PrefetchScalarGridSpec(
            num_scalar_prefetch=1,
            grid=(steps + 1,),
            in_specs=[
                pl.BlockSpec((TILE, width), lambda i, doc: (jnp.minimum(i, steps - 1), 0)),
                whole((1, width)),
                whole(wk.shape),
                whole(wv.shape),
                whole(wb.shape),
            ],
            out_specs=[
                pl.BlockSpec((heads, TILE, DK), lambda i, doc: (0, after(i), 0)),
                pl.BlockSpec((heads, TILE, 2 * DK), lambda i, doc: (0, after(i), 0)),
                pl.BlockSpec((heads, chunks, DK, 2 * DK), lambda i, doc: (0, after(i), 0, 0)),
                whole((heads, DK, 2 * DK)),
                pl.BlockSpec((TILE, DK), lambda i, doc: (jnp.minimum(i, steps - 1), 0)),
            ],
            scratch_shapes=[
                pltpu.VMEM((width, 5 * DK), bf16),
                pltpu.VMEM((2, heads, TILE, DK), bf16),
                pltpu.VMEM((2, heads, TILE, DK), f32),
                pltpu.VMEM((2, TILE, DK), f32),
                pltpu.VMEM((heads, DK, 2 * DK), f32),
                pltpu.VMEM((STEP, STEP), f32),
                pltpu.VMEM((2, STEP, STEP), bf16),
                pltpu.VMEM((len(LEVELS), STEP, STEP), bf16),
            ],
        ),
        out_shape=[
            jax.ShapeDtypeStruct((heads, length, DK), bf16),
            jax.ShapeDtypeStruct((heads, length, 2 * DK), bf16),
            jax.ShapeDtypeStruct((heads, length // DK, DK, 2 * DK), bf16),
            jax.ShapeDtypeStruct((heads, DK, 2 * DK), bf16),
            jax.ShapeDtypeStruct((length, DK), f32),
        ],
        compiler_params=pltpu.CompilerParams(vmem_limit_bytes=56 << 20),
        cost_estimate=pl.CostEstimate(
            flops=2 * length * width * 5 * DK, bytes_accessed=20 << 20, transcendentals=0
        ),
        name="keys_pass",
    )(doc, tokens, gain, wk, wv, wb)


def query_tile(doc, at, x, scale, weights, keys, wu, ps_all, causal, out, carried):
    groups = [(h, g) for g in range(x.shape[0] // STEP) for h in range(2)]
    dm = [doc_masks(doc, at + 4 * g) for g in range(x.shape[0] // STEP)]
    qb, mixed, scores = {}, {}, {}
    for g in range(x.shape[0] // STEP):
        rows = slice(g * STEP, (g + 1) * STEP)
        both = dot(x[rows, :], weights[...]) * scale[rows, 0:1]
        for h in range(2):
            qb[h, g] = unit(both[:, h * DK : (h + 1) * DK]).astype(bf16)
    for h, g in groups:
        rows = slice(g * STEP, (g + 1) * STEP)
        s = dot_nt(qb[h, g], keys[h, rows, :]) * (causal[...] * dm[g][2])
        scores[h, g] = s.astype(bf16)
    for h, g in groups:
        rows = slice(g * STEP, (g + 1) * STEP)
        mixed[h, g] = dot(scores[h, g], wu[h, rows, :])
    for h, g in groups:
        reach = (dm[g][0] * qb[h, g].astype(f32) - mixed[h, g][:, :DK]).astype(bf16)
        for c in range(2):
            rows = slice(c * DK, (c + 1) * DK)
            to = slice(g * STEP + c * DK, g * STEP + (c + 1) * DK)
            seen = dot(reach[rows], ps_all[h, 2 * g + c])
            carried[h, to, :] = seen[:, :DK].astype(bf16)
            out[h, to, :] = mixed[h, g][rows, DK:] + seen[:, DK:]


def query_kernel(doc, x, gain, scale, wq, keys, wu, ps_all, out, carried, weights, causal):
    i = pl.program_id(0)

    @pl.when(i == 0)
    def _():
        weights[...] = scaled_weight(wq, gain)
        row = lax.broadcasted_iota(jnp.int32, (STEP, STEP), 0)
        col = lax.broadcasted_iota(jnp.int32, (STEP, STEP), 1)
        same = (row // DK) == (col // DK)
        causal[...] = jnp.where(same & (row >= col), 1.0, 0.0).astype(f32)

    query_tile(
        doc, i * (x.shape[0] // BLOCK), x, scale, weights, keys, wu, ps_all, causal, out, carried
    )


def query_pass(doc, tokens, gain, scale, wq, keys, wu, ps_all):
    length, width = tokens.shape
    heads = keys.shape[0]
    steps = length // TILE
    whole = lambda shape: pl.BlockSpec(shape, lambda i, doc: (0,) * len(shape))
    part = lambda *tail: pl.BlockSpec((heads, TILE) + tail, lambda i, doc: (0, i) + (0,) * len(tail))
    return pl.pallas_call(
        query_kernel,
        grid_spec=pltpu.PrefetchScalarGridSpec(
            num_scalar_prefetch=1,
            grid=(steps,),
            in_specs=[
                pl.BlockSpec((TILE, width), lambda i, doc: (i, 0)),
                whole((1, width)),
                pl.BlockSpec((TILE, DK), lambda i, doc: (i, 0)),
                whole(wq.shape),
                part(DK),
                part(2 * DK),
                pl.BlockSpec(
                    (heads, TILE // DK, DK, 2 * DK), lambda i, doc: (0, i, 0, 0)
                ),
            ],
            out_specs=[part(DK), part(DK)],
            scratch_shapes=[pltpu.VMEM(wq.shape, bf16), pltpu.VMEM((STEP, STEP), f32)],
        ),
        out_shape=[
            jax.ShapeDtypeStruct((heads, length, DK), f32),
            jax.ShapeDtypeStruct((heads, length, DK), bf16),
        ],
        compiler_params=pltpu.CompilerParams(vmem_limit_bytes=56 << 20),
        cost_estimate=pl.CostEstimate(
            flops=2 * length * width * 3 * DK, bytes_accessed=14 << 20, transcendentals=0
        ),
        name="query_pass",
    )(doc, tokens, gain, scale, wq, keys, wu, ps_all)


def output_kernel(out, carried, incoming, gain, weight, partial):
    columns = []
    for h in range(out.shape[0]):
        o = out[h] + dot(carried[h], incoming[h])
        scale = lax.rsqrt(jnp.mean(o * o, axis=1, keepdims=True) + norm_eps)
        columns.append((o * scale * gain[...]).astype(bf16))
    partial[...] = dot(jnp.concatenate(columns, axis=1), weight[...]).astype(bf16)


def output_pass(out, carried, incoming, gain, weight):
    heads, length, _ = out.shape
    return pl.pallas_call(
        output_kernel,
        grid=(length // STEP,),
        in_specs=[
            pl.BlockSpec((heads, STEP, DK), lambda i: (0, i, 0)),
            pl.BlockSpec((heads, STEP, DK), lambda i: (0, i, 0)),
            pl.BlockSpec(incoming.shape, lambda i: (0, 0, 0)),
            pl.BlockSpec((1, DK), lambda i: (0, 0)),
            pl.BlockSpec(weight.shape, lambda i: (0, 0)),
        ],
        out_specs=pl.BlockSpec((STEP, weight.shape[1]), lambda i: (i, 0)),
        out_shape=jax.ShapeDtypeStruct((length, weight.shape[1]), bf16),
        compiler_params=pltpu.CompilerParams(vmem_limit_bytes=32 << 20),
        name="output_pass",
    )(out, carried, incoming, gain, weight)


def passed_along(block, axis):
    route = [(i, i + 1) for i in range(lax.axis_size(axis) - 1)]
    return lax.ppermute(block, axis, route)


def local(tokens, norm_gain, wq, wk, wv, wb, out_gain, wo, block_doc):
    count = block_doc.shape[0]
    gain = norm_gain[None, :]
    keys, wu, ps_all, ps, scale = keys_pass(block_doc, tokens, gain, wk, wv, wb)
    out, carried = query_pass(block_doc, tokens, gain, scale, wq, keys, wu, ps_all)
    transit, state = ps[:, :, :DK].astype(f32), ps[:, :, DK:].astype(f32)
    first = block_doc[0:1].astype(f32)
    last = block_doc[count - 1 : count].astype(bf16)
    before = passed_along(last, "seq").astype(f32)
    follows = (before[0] == first[0]) & (lax.axis_index("seq") > 0)
    incoming = jnp.zeros_like(state)
    for turn in range(MOST_BLOCKS // count):
        end = state if turn == 0 else jnp.einsum("hde,hef->hdf", transit, incoming) + state
        got = passed_along(end.astype(bf16), "seq").astype(f32)
        incoming = jnp.where(follows, got, 0.0)
    partial = output_pass(out, carried, incoming.astype(bf16), out_gain[None, :], wo)
    return lax.psum_scatter(partial, "head", scatter_dimension=1, tiled=True)


def solution(mesh):
    in_specs = (
        P("seq", None),
        P(),
        P(None, "head"),
        P(None, "head"),
        P(None, "head"),
        P(None, "head"),
        P(),
        P("head", None),
        P("seq"),
    )
    return jax.shard_map(
        local, mesh=mesh, in_specs=in_specs, out_specs=P("seq", "head"), check_vma=False
    )
```

```python
import jax
import jax.numpy as jnp
from jax import lax
from jax.experimental import pallas as pl
from jax.experimental.pallas import tpu as pltpu
from jax.sharding import PartitionSpec as P

norm_eps = 1e-05
key_eps = 1e-06
BLOCK = 64
DK = 128
STEP = 256
TILE = 512
f32 = jnp.float32
bf16 = jnp.bfloat16
LEVELS = (2, 4, 8, 16, 32, 64)


def dot(a, b):
    return jnp.dot(a, b, preferred_element_type=f32)


def dot_nt(a, b):
    return lax.dot_general(a, b, (((1,), (1,)), ((), ())), preferred_element_type=f32)


def dot_tn(a, b):
    return lax.dot_general(a, b, (((0,), (0,)), ((), ())), preferred_element_type=f32)


def unit(values):
    act = values * jax.nn.sigmoid(values)
    return act * lax.rsqrt(jnp.sum(act * act, axis=1, keepdims=True) + key_eps)


def fill_masks(strict, causal, pair, off):
    shape = (STEP, STEP)
    row = lax.broadcasted_iota(jnp.int32, shape, 0)
    col = lax.broadcasted_iota(jnp.int32, shape, 1)
    same = (row // DK) == (col // DK)
    strict[...] = jnp.where(same & (row > col), 1.0, 0.0).astype(f32)
    if causal is not None:
        causal[...] = jnp.where(same & (row >= col), 1.0, 0.0).astype(f32)
    pair[0] = jnp.where((row // 2 == col // 2) & (row > col), 1.0, 0.0).astype(bf16)
    pair[1] = jnp.where(row == col, 1.0, 0.0).astype(bf16)
    for n, s in enumerate(LEVELS):
        hit = (row // (2 * s) == col // (2 * s)) & (row // s > col // s)
        off[n] = jnp.where(hit, 1.0, 0.0).astype(bf16)


def scaled_weight(weight, gain):
    column = jnp.transpose(jnp.broadcast_to(gain[...], (DK, gain.shape[1])))
    parts = [
        weight[:, n * DK : (n + 1) * DK].astype(f32) * column for n in range(weight.shape[1] // DK)
    ]
    return jnp.concatenate(parts, axis=1).astype(bf16)


def doc_masks(doc, at):
    d = [doc[at + j] for j in range(4)]
    before = doc[jnp.maximum(at - 1, 0)]
    link = [
        jnp.where((before == d[0]) | (at == 0), 1.0, 0.0).astype(f32),
        jnp.where(d[1] == d[2], 1.0, 0.0).astype(f32),
    ]
    join = [
        jnp.where(d[0] == d[1], 1.0, 0.0).astype(f32),
        jnp.where(d[2] == d[3], 1.0, 0.0).astype(f32),
    ]
    row = lax.broadcasted_iota(jnp.int32, (STEP, 1), 0)
    second = (row % DK) >= BLOCK
    join_r = jnp.where(row >= DK, join[1], join[0])
    link_r = jnp.where(row >= DK, link[1], link[0])
    enters = jnp.where(second, link_r * join_r, link_r)
    leaves = jnp.where(second, 1.0, join_r)
    cross = jnp.where(second, join_r, 1.0)
    col = lax.broadcasted_iota(jnp.int32, (1, STEP), 1)
    full = jnp.where((col % DK) < BLOCK, cross, 1.0)
    return enters, leaves, full, [link[c] * join[c] for c in range(2)]


def interleave(main, side, every):
    count = 0
    for _ in main:
        count += 1
        if count % every == 0:
            next(side, None)
    for _ in side:
        pass


def project_keys(x, scale_out, weights, kbuf, vbuf, bbuf, slot):
    halves = x.shape[0] // STEP
    scales = []
    for m in range(halves):
        rows = slice(m * STEP, (m + 1) * STEP)
        floats = x[rows, :].astype(f32)
        r = lax.rsqrt(jnp.mean(floats * floats, axis=1, keepdims=True) + norm_eps)
        scales.append(r)
        scale_out[rows, :] = jnp.broadcast_to(r, (STEP, DK))
        yield
        b = dot(x[rows, :], weights[:, 4 * DK :]) * r
        bbuf[slot, rows, :] = jax.nn.sigmoid(b)
        yield
        for h in range(2):
            kv = dot(x[rows, :], weights[:, 2 * h * DK : 2 * (h + 1) * DK]) * r
            kbuf[slot, h, rows, :] = unit(kv[:, :DK]).astype(bf16)
            vbuf[slot, h, rows, :] = kv[:, DK:]
            yield


def solve_keys(doc, at, kbuf, vbuf, bbuf, slot, ps, masks, wu_out, ps_all):
    strict, pair, off, wu_buf, end_buf = masks
    halves = kbuf.shape[2] // STEP
    groups = [(h, g) for g in range(halves) for h in range(2)]
    dm = [doc_masks(doc, at + 4 * g) for g in range(halves)]
    keys, a_hi, a_lo, xb, t, right, y, wu = {}, {}, {}, {}, {}, {}, {}, {}
    beta = {}
    for h, g in groups:
        rows = slice(g * STEP, (g + 1) * STEP)
        keys[h, g] = kbuf[slot, h, rows, :]
        beta[h, g] = bbuf[slot, rows, h : h + 1]
        a = dot_nt(keys[h, g], keys[h, g]) * beta[h, g] * (strict[...] * dm[g][2])
        hi = a.astype(bf16)
        a_hi[h, g] = hi
        a_lo[h, g] = (a - hi.astype(f32)).astype(bf16)
        xb[h, g] = pair[1] - hi * pair[0]
        yield
    for n in range(len(LEVELS)):
        for at_group in groups:
            t[at_group] = dot(a_hi[at_group] * off[n], xb[at_group]).astype(bf16)
        yield
        for at_group in groups:
            xb[at_group] = xb[at_group] - dot(xb[at_group], t[at_group]).astype(bf16)
        yield
    for h, g in groups:
        rows = slice(g * STEP, (g + 1) * STEP)
        b = beta[h, g]
        right[h, g] = jnp.concatenate(
            [(b * dm[g][0]) * keys[h, g].astype(f32), b * vbuf[slot, h, rows, :]], axis=1
        )
        y[h, g] = dot(xb[h, g], right[h, g].astype(bf16)).astype(bf16)
    yield
    left = {}
    for k in groups:
        rest = right[k] - y[k].astype(f32) - dot(a_hi[k], y[k]) - dot(a_lo[k], y[k])
        left[k] = rest.astype(bf16)
    yield
    for h, g in groups:
        wu[h, g] = (y[h, g].astype(f32) + dot(xb[h, g], left[h, g])).astype(bf16)
        wu_out[h, g * STEP : (g + 1) * STEP, :] = wu[h, g]
    yield
    step = {}
    for h, g in groups:
        k_end = (keys[h, g].astype(f32) * dm[g][1]).astype(bf16)
        for c in range(2):
            rows = slice(c * DK, (c + 1) * DK)
            step[h, g, c] = dot_tn(k_end[rows], wu[h, g][rows])
    yield
    for g in range(halves):
        for c in range(2):
            for h in range(2):
                state = ps[h]
                sb = state.astype(bf16)
                ps_all[h, 2 * g + c] = sb
                move = step[h, g, c]
                moved = dot(move[:, :DK].astype(bf16), sb)
                gain = jnp.concatenate([jnp.zeros((DK, DK), f32), move[:, DK:]], axis=1)
                ps[h] = dm[g][3][c] * state - moved + gain
            yield


def keys_kernel(
    doc, x, gain, wk, wv, wb, k_out, wu_out, ps_all, ps_end, scale_out,
    weights, kbuf, vbuf, bbuf, ps, strict, pair, off,
):
    i, last = pl.program_id(0), pl.num_programs(0) - 1
    tile = x.shape[0]
    blocks = tile // BLOCK

    def project():
        return project_keys(x, scale_out, weights, kbuf, vbuf, bbuf, i % 2)

    def solve():
        slot = (i + 1) % 2
        k_out[...] = kbuf[slot]
        return solve_keys(
            doc, (i - 1) * blocks, kbuf, vbuf, bbuf, slot, ps,
            (strict, pair, off, None, None), wu_out, ps_all,
        )

    @pl.when(i == 0)
    def _():
        fill_masks(strict, None, pair, off)
        sk, sv = scaled_weight(wk, gain), scaled_weight(wv, gain)
        for h in range(2):
            weights[:, 2 * h * DK : (2 * h + 1) * DK] = sk[:, h * DK : (h + 1) * DK]
            weights[:, (2 * h + 1) * DK : (2 * h + 2) * DK] = sv[:, h * DK : (h + 1) * DK]
        wide = jnp.concatenate(
            [wb[...], jnp.zeros((wb.shape[0], DK - wb.shape[1]), bf16)], axis=1
        )
        weights[:, 4 * DK :] = scaled_weight(wide, gain)
        row = lax.broadcasted_iota(jnp.int32, (DK, 2 * DK), 0)
        col = lax.broadcasted_iota(jnp.int32, (DK, 2 * DK), 1)
        for h in range(2):
            ps[h] = jnp.where(row == col, 1.0, 0.0).astype(f32)
        for _ in project():
            pass

    @pl.when((i > 0) & (i < last))
    def _():
        interleave(solve(), project(), 2)

    @pl.when(i == last)
    def _():
        for _ in solve():
            pass
        for h in range(2):
            ps_end[h] = ps[h].astype(bf16)


def keys_pass(doc, tokens, gain, wk, wv, wb):
    length, width = tokens.shape
    heads = wb.shape[1]
    steps = length // TILE
    chunks = TILE // DK
    after = lambda i: jnp.maximum(i - 1, 0)
    whole = lambda shape: pl.BlockSpec(shape, lambda i, doc: (0,) * len(shape))
    return pl.pallas_call(
        keys_kernel,
        grid_spec=pltpu.PrefetchScalarGridSpec(
            num_scalar_prefetch=1,
            grid=(steps + 1,),
            in_specs=[
                pl.BlockSpec((TILE, width), lambda i, doc: (jnp.minimum(i, steps - 1), 0)),
                whole((1, width)),
                whole(wk.shape),
                whole(wv.shape),
                whole(wb.shape),
            ],
            out_specs=[
                pl.BlockSpec((heads, TILE, DK), lambda i, doc: (0, after(i), 0)),
                pl.BlockSpec((heads, TILE, 2 * DK), lambda i, doc: (0, after(i), 0)),
                pl.BlockSpec((heads, chunks, DK, 2 * DK), lambda i, doc: (0, after(i), 0, 0)),
                whole((heads, DK, 2 * DK)),
                pl.BlockSpec((TILE, DK), lambda i, doc: (jnp.minimum(i, steps - 1), 0)),
            ],
            scratch_shapes=[
                pltpu.VMEM((width, 5 * DK), bf16),
                pltpu.VMEM((2, heads, TILE, DK), bf16),
                pltpu.VMEM((2, heads, TILE, DK), f32),
                pltpu.VMEM((2, TILE, DK), f32),
                pltpu.VMEM((heads, DK, 2 * DK), f32),
                pltpu.VMEM((STEP, STEP), f32),
                pltpu.VMEM((2, STEP, STEP), bf16),
                pltpu.VMEM((len(LEVELS), STEP, STEP), bf16),
            ],
        ),
        out_shape=[
            jax.ShapeDtypeStruct((heads, length, DK), bf16),
            jax.ShapeDtypeStruct((heads, length, 2 * DK), bf16),
            jax.ShapeDtypeStruct((heads, length // DK, DK, 2 * DK), bf16),
            jax.ShapeDtypeStruct((heads, DK, 2 * DK), bf16),
            jax.ShapeDtypeStruct((length, DK), f32),
        ],
        compiler_params=pltpu.CompilerParams(vmem_limit_bytes=56 << 20),
        cost_estimate=pl.CostEstimate(
            flops=2 * length * width * 5 * DK, bytes_accessed=20 << 20, transcendentals=0
        ),
        name="keys_pass",
    )(doc, tokens, gain, wk, wv, wb)


def query_tile(doc, at, x, scale, weights, keys, wu, ps_all, causal, out, carried):
    groups = [(h, g) for g in range(x.shape[0] // STEP) for h in range(2)]
    dm = [doc_masks(doc, at + 4 * g) for g in range(x.shape[0] // STEP)]
    qb, mixed, scores = {}, {}, {}
    for g in range(x.shape[0] // STEP):
        rows = slice(g * STEP, (g + 1) * STEP)
        both = dot(x[rows, :], weights[...]) * scale[rows, 0:1]
        for h in range(2):
            qb[h, g] = unit(both[:, h * DK : (h + 1) * DK]).astype(bf16)
    for h, g in groups:
        rows = slice(g * STEP, (g + 1) * STEP)
        s = dot_nt(qb[h, g], keys[h, rows, :]) * (causal[...] * dm[g][2])
        scores[h, g] = s.astype(bf16)
    for h, g in groups:
        rows = slice(g * STEP, (g + 1) * STEP)
        mixed[h, g] = dot(scores[h, g], wu[h, rows, :])
    for h, g in groups:
        reach = (dm[g][0] * qb[h, g].astype(f32) - mixed[h, g][:, :DK]).astype(bf16)
        for c in range(2):
            rows = slice(c * DK, (c + 1) * DK)
            to = slice(g * STEP + c * DK, g * STEP + (c + 1) * DK)
            seen = dot(reach[rows], ps_all[h, 2 * g + c])
            carried[h, to, :] = seen[:, :DK].astype(bf16)
            out[h, to, :] = mixed[h, g][rows, DK:] + seen[:, DK:]


def peer(s, h):
    return dict(device_id=(s, h), device_id_type=pl.DeviceIdType.MESH)


def join(first, then, follows):
    moved = jnp.where(follows, dot(then[:, :DK], first), 0.0)
    gain = jnp.concatenate([jnp.zeros((DK, DK), f32), then[:, DK:].astype(f32)], axis=1)
    return (moved + gain).astype(bf16)


def query_kernel(
    doc, x, gain, scale, wq, keys, wu, ps_all, ps, out_gain, result,
    weights, causal, out, carried, own, near, three, far1, far4, send, recv,
):
    i, last = pl.program_id(0), pl.num_programs(0) - 1
    tile = x.shape[0]
    heads = keys.shape[0]
    count = result.shape[0] // BLOCK
    s, h = lax.axis_index("seq"), lax.axis_index("head")
    n = lax.axis_size("seq")
    to = lambda d: peer(lax.rem(s + d + n, n), h)
    foot = heads * DK

    def move(src, dst, at, d):
        return pltpu.make_async_remote_copy(
            src_ref=src, dst_ref=dst, send_sem=send.at[at], recv_sem=recv.at[at], **to(d)
        )

    first_copies = [move(own, near.at[0], 0, 1), move(own, near.at[1], 1, 2)]
    second_copies = [
        move(three, far1, 2, 1),
        move(three.at[:, DK:], far4, 3, 4),
    ]

    @pl.when(i == 0)
    def _():
        barrier = pltpu.get_barrier_semaphore()
        for d in (1, -1, 2, -2, 4, -4):
            pl.semaphore_signal(barrier, inc=1, **to(d))
        for k in range(heads):
            own[k * DK : (k + 1) * DK, :] = ps[k]
        own[foot:, :DK] = jnp.full((16, DK), doc[0].astype(f32)).astype(bf16)
        own[foot:, DK:] = jnp.full((16, DK), doc[count - 1].astype(f32)).astype(bf16)
        pl.semaphore_wait(barrier, 6)
        for copy in first_copies:
            copy.start()
        weights[...] = scaled_weight(wq, gain)
        row = lax.broadcasted_iota(jnp.int32, (STEP, STEP), 0)
        col = lax.broadcasted_iota(jnp.int32, (STEP, STEP), 1)
        same = (row // DK) == (col // DK)
        causal[...] = jnp.where(same & (row >= col), 1.0, 0.0).astype(f32)

    @pl.when(i == last)
    def _():
        for copy in first_copies:
            copy.wait()
        first_own, last_before = own[foot : foot + 1, 0:1], near[0, foot : foot + 1, DK : DK + 1]
        first_before, last_two = near[0, foot : foot + 1, 0:1], near[1, foot : foot + 1, DK : DK + 1]
        for k in range(heads):
            rows = slice(k * DK, (k + 1) * DK)
            two = join(near[1, rows, :], near[0, rows, :], (last_two == first_before) & (s >= 2))
            three[rows, :] = join(two, own[rows, :], (last_before == first_own) & (s >= 1))
        three[foot:, :DK] = near[1, foot:, :DK]
        three[foot:, DK:] = own[foot:, DK:]
        for copy in second_copies:
            copy.start()

    at_tile = pl.ds(pl.multiple_of(i * tile, tile), tile)
    query_tile(
        doc, i * (tile // BLOCK), x, scale, weights, keys, wu, ps_all, causal,
        out.at[:, at_tile, :], carried.at[:, at_tile, :],
    )

    @pl.when(i == last)
    def _():
        for copy in second_copies:
            copy.wait()
        first_own, last_before = own[foot : foot + 1, 0:1], far1[foot : foot + 1, DK : DK + 1]
        first_three, last_four = far1[foot : foot + 1, 0:1], far4[foot : foot + 1, 0:1]
        for k in range(heads):
            rows = slice(k * DK, (k + 1) * DK)
            older = jnp.where(
                (last_four == first_three) & (s >= 4), dot(far1[rows, :DK], far4[rows, :]), 0.0
            )
            state = older + far1[rows, DK:].astype(f32)
            entering = jnp.where((last_before == first_own) & (s >= 1), state, 0.0).astype(bf16)
            for g in range(result.shape[0] // STEP):
                part = slice(g * STEP, (g + 1) * STEP)
                o = out[k, part, :] + dot(carried[k, part, :], entering)
                r = lax.rsqrt(jnp.mean(o * o, axis=1, keepdims=True) + norm_eps)
                result[part, k * DK : (k + 1) * DK] = (o * r * out_gain[...]).astype(bf16)


def query_pass(doc, tokens, gain, scale, wq, keys, wu, ps_all, ps, out_gain):
    length, width = tokens.shape
    heads = keys.shape[0]
    steps = length // TILE
    whole = lambda shape: pl.BlockSpec(shape, lambda i, doc: (0,) * len(shape))
    part = lambda *tail: pl.BlockSpec((heads, TILE) + tail, lambda i, doc: (0, i) + (0,) * len(tail))
    message = (heads * DK + 16, 2 * DK)
    return pl.pallas_call(
        query_kernel,
        grid_spec=pltpu.PrefetchScalarGridSpec(
            num_scalar_prefetch=1,
            grid=(steps,),
            in_specs=[
                pl.BlockSpec((TILE, width), lambda i, doc: (i, 0)),
                whole((1, width)),
                pl.BlockSpec((TILE, DK), lambda i, doc: (i, 0)),
                whole(wq.shape),
                part(DK),
                part(2 * DK),
                pl.BlockSpec((heads, TILE // DK, DK, 2 * DK), lambda i, doc: (0, i, 0, 0)),
                whole(ps.shape),
                whole(out_gain.shape),
            ],
            out_specs=whole((length, heads * DK)),
            scratch_shapes=[
                pltpu.VMEM(wq.shape, bf16),
                pltpu.VMEM((STEP, STEP), f32),
                pltpu.VMEM((heads, length, DK), f32),
                pltpu.VMEM((heads, length, DK), bf16),
                pltpu.VMEM(message, bf16),
                pltpu.VMEM((2,) + message, bf16),
                pltpu.VMEM(message, bf16),
                pltpu.VMEM(message, bf16),
                pltpu.VMEM((message[0], DK), bf16),
                pltpu.SemaphoreType.DMA((4,)),
                pltpu.SemaphoreType.DMA((4,)),
            ],
        ),
        out_shape=jax.ShapeDtypeStruct((length, heads * DK), bf16),
        compiler_params=pltpu.CompilerParams(
            vmem_limit_bytes=56 << 20, collective_id=0, has_side_effects=True
        ),
        cost_estimate=pl.CostEstimate(
            flops=2 * length * width * 3 * DK, bytes_accessed=14 << 20, transcendentals=0
        ),
        name="query_pass",
    )(doc, tokens, gain, scale, wq, keys, wu, ps_all, ps, out_gain)


SUBS = 2


def mix_kernel(
    normed, full, out, gath, w, obuf,
    w_sem, there_s, there_r, share_s, share_r, back_s, back_r,
):
    s, h = lax.axis_index("seq"), lax.axis_index("head")
    chips = lax.axis_size("head") // 2
    y, c = h // 2, lax.rem(h, 2)
    length, width = normed.shape
    part = length // chips
    sub = part // SUBS
    chip = lambda d: lax.rem(y + d + chips, chips)
    away = lambda d: peer(s, chip(d) * 2 + c)
    beside = peer(s, y * 2 + 1 - c)

    def columns(chip_at, core):
        return pl.ds(pl.multiple_of((chip_at * 2 + core) * width, width), width)

    def rows(chip_at, r):
        return pl.ds(pl.multiple_of(chip_at * part + r * sub, sub), sub)

    barrier = pltpu.get_barrier_semaphore()
    for d in range(1, chips):
        pl.semaphore_signal(barrier, inc=1, **away(d))
    pl.semaphore_signal(barrier, inc=1, **beside)
    loads = []
    for d in range(chips):
        loads.append(
            pltpu.make_async_copy(
                full.at[:, columns(chip(d), c)], w.at[:, d * width : (d + 1) * width], w_sem.at[d]
            )
        )
    for load in loads:
        load.start()
    pl.semaphore_wait(barrier, chips)

    def there(r, d):
        return pltpu.make_async_remote_copy(
            src_ref=normed.at[rows(chip(d), r), :],
            dst_ref=gath.at[r * sub : (r + 1) * sub, columns(y, c)],
            send_sem=there_s.at[r, d],
            recv_sem=there_r.at[r, d],
            **away(d),
        )

    def share(r, d):
        at = (slice(r * sub, (r + 1) * sub), columns(chip(-d), c))
        src = normed.at[rows(y, r), :] if d == 0 else gath.at[at]
        return pltpu.make_async_remote_copy(
            src_ref=src,
            dst_ref=gath.at[at],
            send_sem=share_s.at[r, d],
            recv_sem=share_r.at[r, d],
            **beside,
        )

    def back(r, d):
        return pltpu.make_async_remote_copy(
            src_ref=obuf.at[r, d],
            dst_ref=out.at[rows(y, r), :],
            send_sem=back_s.at[r, d],
            recv_sem=back_r.at[r, d],
            **away(d),
        )

    order = [2, 1, 3]
    for r in range(SUBS):
        for d in order:
            there(r, d).start()
    for r in range(SUBS):
        share(r, 0).start()
        gath[r * sub : (r + 1) * sub, columns(y, c)] = normed[rows(y, r), :]
    for r in range(SUBS):
        for d in [1, 3, 2]:
            there(r, d).wait_recv()
            share(r, d).start()
        for d in range(chips):
            share(r, d).wait_recv()
        if r == 0:
            for load in loads:
                load.wait()
        block = gath[r * sub : (r + 1) * sub, :]
        for d in order:
            obuf[r, d] = dot(block, w[:, d * width : (d + 1) * width]).astype(bf16)
            back(r, d).start()
        out[rows(y, r), :] = dot(block, w[:, :width]).astype(bf16)
    for r in range(SUBS):
        for d in order:
            there(r, d).wait_send()
        for d in range(chips):
            share(r, d).wait_send()
    for r in range(SUBS):
        for d in order:
            back(r, d).wait()


def mix_pass(normed, full):
    length, width = normed.shape
    chips = full.shape[0] // width // 2
    part = length // chips
    sub = part // SUBS
    dma = lambda *shape: pltpu.SemaphoreType.DMA(shape)
    vmem = pl.BlockSpec(memory_space=pltpu.VMEM)
    return pl.pallas_call(
        mix_kernel,
        in_specs=[vmem, pl.BlockSpec(memory_space=pl.ANY)],
        out_specs=vmem,
        out_shape=jax.ShapeDtypeStruct((length, width), bf16),
        scratch_shapes=[
            pltpu.VMEM((part, full.shape[0]), bf16),
            pltpu.VMEM((full.shape[0], chips * width), bf16),
            pltpu.VMEM((SUBS, chips, sub, width), bf16),
            dma(chips),
            dma(SUBS, chips),
            dma(SUBS, chips),
            dma(SUBS, chips),
            dma(SUBS, chips),
            dma(SUBS, chips),
            dma(SUBS, chips),
        ],
        compiler_params=pltpu.CompilerParams(
            vmem_limit_bytes=56 << 20, collective_id=1, has_side_effects=True
        ),
        name="mix_pass",
    )(normed, full)


def local(tokens, norm_gain, wq, wk, wv, wb, out_gain, wo, block_doc):
    gain = norm_gain[None, :]
    full = lax.all_gather(wo, "head", axis=0, tiled=True)
    keys, wu, ps_all, ps, scale = keys_pass(block_doc, tokens, gain, wk, wv, wb)
    normed = query_pass(
        block_doc, tokens, gain, scale, wq, keys, wu, ps_all, ps, out_gain[None, :]
    )
    return mix_pass(normed, full)


def solution(mesh):
    in_specs = (
        P("seq", None),
        P(),
        P(None, "head"),
        P(None, "head"),
        P(None, "head"),
        P(None, "head"),
        P(),
        P("head", None),
        P("seq"),
    )
    return jax.shard_map(
        local, mesh=mesh, in_specs=in_specs, out_specs=P("seq", "head"), check_vma=False
    )
```

```python
import jax
import jax.numpy as jnp
from jax import lax
from jax.experimental import pallas as pl
from jax.experimental.pallas import tpu as pltpu
from jax.sharding import PartitionSpec as P

norm_eps = 1e-05
key_eps = 1e-06
BLOCK = 64
DK = 128
STEP = 256
TILE = 512
SIDE = 4
SPREAD_AT = 2
SUBS = 2
f32 = jnp.float32
bf16 = jnp.bfloat16
LEVELS = (2, 4, 8, 16, 32, 64)


def dot(a, b):
    return jnp.dot(a, b, preferred_element_type=f32)


def dot_nt(a, b):
    return lax.dot_general(a, b, (((1,), (1,)), ((), ())), preferred_element_type=f32)


def dot_tn(a, b):
    return lax.dot_general(a, b, (((0,), (0,)), ((), ())), preferred_element_type=f32)


def unit(values):
    act = values * jax.nn.sigmoid(values)
    return act * lax.rsqrt(jnp.sum(act * act, axis=1, keepdims=True) + key_eps)


def peer(s, h):
    return dict(device_id=(s, h), device_id_type=pl.DeviceIdType.MESH)


def fill_masks(strict, causal, pair, off):
    shape = (STEP, STEP)
    row = lax.broadcasted_iota(jnp.int32, shape, 0)
    col = lax.broadcasted_iota(jnp.int32, shape, 1)
    same = (row // DK) == (col // DK)
    strict[...] = jnp.where(same & (row > col), 1.0, 0.0).astype(f32)
    causal[...] = jnp.where(same & (row >= col), 1.0, 0.0).astype(f32)
    pair[0] = jnp.where((row // 2 == col // 2) & (row > col), 1.0, 0.0).astype(bf16)
    pair[1] = jnp.where(row == col, 1.0, 0.0).astype(bf16)
    for n, s in enumerate(LEVELS):
        hit = (row // (2 * s) == col // (2 * s)) & (row // s > col // s)
        off[n] = jnp.where(hit, 1.0, 0.0).astype(bf16)


def scaled_weight(weight, gain):
    column = jnp.transpose(jnp.broadcast_to(gain[...], (DK, gain.shape[1])))
    parts = [
        weight[:, n * DK : (n + 1) * DK].astype(f32) * column for n in range(weight.shape[1] // DK)
    ]
    return jnp.concatenate(parts, axis=1).astype(bf16)


def doc_masks(doc, at):
    d = [doc[at + j] for j in range(4)]
    before = doc[jnp.maximum(at - 1, 0)]
    link = [
        jnp.where((before == d[0]) | (at == 0), 1.0, 0.0).astype(f32),
        jnp.where(d[1] == d[2], 1.0, 0.0).astype(f32),
    ]
    join = [
        jnp.where(d[0] == d[1], 1.0, 0.0).astype(f32),
        jnp.where(d[2] == d[3], 1.0, 0.0).astype(f32),
    ]
    row = lax.broadcasted_iota(jnp.int32, (STEP, 1), 0)
    second = (row % DK) >= BLOCK
    join_r = jnp.where(row >= DK, join[1], join[0])
    link_r = jnp.where(row >= DK, link[1], link[0])
    enters = jnp.where(second, link_r * join_r, link_r)
    leaves = jnp.where(second, 1.0, join_r)
    cross = jnp.where(second, join_r, 1.0)
    col = lax.broadcasted_iota(jnp.int32, (1, STEP), 1)
    full = jnp.where((col % DK) < BLOCK, cross, 1.0)
    return enters, leaves, full, [link[c] * join[c] for c in range(2)]


def interleave(main, side, every):
    count = 0
    for _ in main:
        count += 1
        if count % every == 0:
            next(side, None)
    for _ in side:
        pass


def project_keys(x, scale_out, weights, keys_at, vbuf, bbuf, slot):
    halves = x.shape[0] // STEP
    scales = []
    for m in range(halves):
        rows = slice(m * STEP, (m + 1) * STEP)
        floats = x[rows, :].astype(f32)
        r = lax.rsqrt(jnp.mean(floats * floats, axis=1, keepdims=True) + norm_eps)
        scales.append(r)
        scale_out[rows, :] = jnp.broadcast_to(r, (STEP, DK))
        yield
        b = dot(x[rows, :], weights[:, 4 * DK :]) * r
        bbuf[slot, rows, :] = jax.nn.sigmoid(b)
        yield
        for h in range(2):
            kv = dot(x[rows, :], weights[:, 2 * h * DK : 2 * (h + 1) * DK]) * r
            keys_at[h, rows, :] = unit(kv[:, :DK]).astype(bf16)
            vbuf[slot, h, rows, :] = kv[:, DK:]
            yield


def solve_keys(doc, at, keys_at, vbuf, bbuf, slot, ps, masks, wu_out, ps_all):
    strict, pair, off = masks
    halves = keys_at.shape[1] // STEP
    groups = [(h, g) for g in range(halves) for h in range(2)]
    dm = [doc_masks(doc, at + 4 * g) for g in range(halves)]
    keys, a_hi, a_lo, xb, t, right, y, wu = {}, {}, {}, {}, {}, {}, {}, {}
    beta = {}
    for h, g in groups:
        rows = slice(g * STEP, (g + 1) * STEP)
        keys[h, g] = keys_at[h, rows, :]
        beta[h, g] = bbuf[slot, rows, h : h + 1]
        a = dot_nt(keys[h, g], keys[h, g]) * beta[h, g] * (strict[...] * dm[g][2])
        hi = a.astype(bf16)
        a_hi[h, g] = hi
        a_lo[h, g] = (a - hi.astype(f32)).astype(bf16)
        xb[h, g] = pair[1] - hi * pair[0]
        yield
    for n in range(len(LEVELS)):
        for at_group in groups:
            t[at_group] = dot(a_hi[at_group] * off[n], xb[at_group]).astype(bf16)
        yield
        for at_group in groups:
            xb[at_group] = xb[at_group] - dot(xb[at_group], t[at_group]).astype(bf16)
        yield
    for h, g in groups:
        rows = slice(g * STEP, (g + 1) * STEP)
        b = beta[h, g]
        right[h, g] = jnp.concatenate(
            [(b * dm[g][0]) * keys[h, g].astype(f32), b * vbuf[slot, h, rows, :]], axis=1
        )
        y[h, g] = dot(xb[h, g], right[h, g].astype(bf16)).astype(bf16)
    yield
    left = {}
    for k in groups:
        rest = right[k] - y[k].astype(f32) - dot(a_hi[k], y[k]) - dot(a_lo[k], y[k])
        left[k] = rest.astype(bf16)
    yield
    for h, g in groups:
        wu[h, g] = (y[h, g].astype(f32) + dot(xb[h, g], left[h, g])).astype(bf16)
        wu_out[h, g * STEP : (g + 1) * STEP, :] = wu[h, g]
    yield
    step = {}
    for h, g in groups:
        k_end = (keys[h, g].astype(f32) * dm[g][1]).astype(bf16)
        for c in range(2):
            rows = slice(c * DK, (c + 1) * DK)
            step[h, g, c] = dot_tn(k_end[rows], wu[h, g][rows])
    yield
    for g in range(halves):
        for c in range(2):
            for h in range(2):
                state = ps[h]
                sb = state.astype(bf16)
                ps_all[h, 2 * g + c] = sb
                move = step[h, g, c]
                moved = dot(move[:, :DK].astype(bf16), sb)
                gain = jnp.concatenate([jnp.zeros((DK, DK), f32), move[:, DK:]], axis=1)
                ps[h] = dm[g][3][c] * state - moved + gain
            yield


def query_tile(doc, at, x, scale, weights, keys, wu, ps_all, causal, out, carried):
    groups = [(h, g) for g in range(x.shape[0] // STEP) for h in range(2)]
    dm = [doc_masks(doc, at + 4 * g) for g in range(x.shape[0] // STEP)]
    qb, mixed, scores = {}, {}, {}
    for g in range(x.shape[0] // STEP):
        rows = slice(g * STEP, (g + 1) * STEP)
        both = dot(x[rows, :], weights[...]) * scale[rows, 0:1]
        for h in range(2):
            qb[h, g] = unit(both[:, h * DK : (h + 1) * DK]).astype(bf16)
    for h, g in groups:
        rows = slice(g * STEP, (g + 1) * STEP)
        s = dot_nt(qb[h, g], keys[h, rows, :]) * (causal[...] * dm[g][2])
        scores[h, g] = s.astype(bf16)
    for h, g in groups:
        rows = slice(g * STEP, (g + 1) * STEP)
        mixed[h, g] = dot(scores[h, g], wu[h, rows, :])
    for h, g in groups:
        reach = (dm[g][0] * qb[h, g].astype(f32) - mixed[h, g][:, :DK]).astype(bf16)
        for c in range(2):
            rows = slice(c * DK, (c + 1) * DK)
            to = slice(g * STEP + c * DK, g * STEP + (c + 1) * DK)
            seen = dot(reach[rows], ps_all[h, 2 * g + c])
            carried[h, to, :] = seen[:, :DK].astype(bf16)
            out[h, to, :] = mixed[h, g][rows, DK:] + seen[:, DK:]


class Place:
    def __init__(self):
        self.s, h = lax.axis_index("seq"), lax.axis_index("head")
        self.length = lax.axis_size("seq")
        self.chips = lax.axis_size("head") // 2
        self.y, self.c = h // 2, lax.rem(h, 2)
        self.outer, self.inner = self.s // SIDE, lax.rem(self.s, SIDE)

    def later(self, d):
        return peer(lax.rem(self.s + d + self.length, self.length), self.y * 2 + self.c)

    def chip(self, d, core):
        return peer(self.s, lax.rem(self.y + d + self.chips, self.chips) * 2 + core)

    def beside(self):
        return self.chip(0, 1 - self.c)

    def along(self, axis, d):
        if axis == 0:
            s = lax.rem(self.outer + d + SIDE, SIDE) * SIDE + self.inner
        else:
            s = self.outer * SIDE + lax.rem(self.inner + d + SIDE, SIDE)
        return peer(s, self.y * 2 + self.c)

    def peers(self):
        found = [self.chip(d, core) for d in range(1, self.chips) for core in range(2)]
        found.append(self.beside())
        found += [self.along(a, d) for a in range(2) for d in range(1, SIDE)]
        return found + [self.later(d) for d in (1, -1, 2, -2, 4, -4)]


class WeightGather:
    def __init__(self, me, wo, w, over_s, over_r, near_s, ring_s, ring_r):
        self.me, self.wo, self.w = me, wo, w
        self.over_s, self.over_r, self.near_s = over_s, over_r, near_s
        self.ring_s, self.ring_r = ring_s, ring_r
        self.depth, self.half = w.shape[1], w.shape[2]
        self.quarter, self.wide = self.depth // SIDE, self.half // 2

    def rows(self, axis):
        q = self.me.outer if axis == 0 else self.me.inner
        return pl.ds(pl.multiple_of(q * self.quarter, self.quarter), self.quarter)

    def over(self, d, core, axis, origin):
        start = core * self.half + axis * self.wide
        block = (self.me.chips - d) * 2 + origin
        return pltpu.make_async_remote_copy(
            src_ref=self.wo.at[self.rows(axis), start : start + self.wide],
            dst_ref=self.w.at[block, self.rows(axis), axis * self.wide : (axis + 1) * self.wide],
            send_sem=self.over_s.at[d - 1, core, axis],
            recv_sem=self.over_r.at[d - 1, origin, axis],
            **self.me.chip(d, core),
        )

    def columns(self, core):
        return pl.ds(pl.multiple_of(core * self.half, self.half), self.half)

    def pair(self):
        return pltpu.make_async_remote_copy(
            src_ref=self.wo.at[:, self.columns(1 - self.me.c)],
            dst_ref=self.w.at[self.me.c],
            send_sem=self.near_s.at[0],
            recv_sem=self.near_s.at[1],
            **self.me.beside(),
        )

    def own(self):
        return pltpu.make_async_copy(
            self.wo.at[:, self.columns(self.me.c)], self.w.at[self.me.c], self.near_s.at[2]
        )

    def ring(self, axis, d):
        at = self.w.at[2:, self.rows(axis), axis * self.wide : (axis + 1) * self.wide]
        return pltpu.make_async_remote_copy(
            src_ref=at,
            dst_ref=at,
            send_sem=self.ring_s.at[axis, d - 1],
            recv_sem=self.ring_r.at[axis, d - 1],
            **self.me.along(axis, d),
        )

    def each_over(self):
        return [(d, k, a) for d in (2, 1, 3) for k in range(2) for a in range(2)]

    def each_ring(self):
        return [(a, d) for d in (2, 1, 3) for a in range(2)]

    def begin(self):
        for d, core, axis in self.each_over():
            self.over(d, core, axis, self.me.c).start()
        self.pair().start()
        self.own().start()

    def spread(self):
        for d, core, axis in self.each_over():
            self.over(d, core, axis, core).wait_recv()
        for at in self.each_ring():
            self.ring(*at).start()

    def finish(self):
        for d, core, axis in self.each_over():
            self.over(d, core, axis, self.me.c).wait_send()
        self.pair().wait()
        self.own().wait()
        for at in self.each_ring():
            self.ring(*at).wait()


def join(first, then, follows):
    moved = jnp.where(follows, dot(then[:, :DK], first), 0.0)
    gain = jnp.concatenate([jnp.zeros((DK, DK), f32), then[:, DK:].astype(f32)], axis=1)
    return (moved + gain).astype(bf16)


class StateExchange:
    def __init__(self, me, own, near, three, far1, far4, send, recv):
        self.me = me
        self.own, self.near, self.three, self.far1, self.far4 = own, near, three, far1, far4
        self.send, self.recv = send, recv
        self.foot = own.shape[0] - 16

    def move(self, src, dst, at, d):
        return pltpu.make_async_remote_copy(
            src_ref=src, dst_ref=dst, send_sem=self.send.at[at], recv_sem=self.recv.at[at],
            **self.me.later(d),
        )

    def first_round(self):
        return [self.move(self.own, self.near.at[0], 0, 1), self.move(self.own, self.near.at[1], 1, 2)]

    def second_round(self):
        return [
            self.move(self.three, self.far1, 2, 1),
            self.move(self.three.at[:, DK:], self.far4, 3, 4),
        ]

    def begin(self, ps, first_doc, last_doc):
        foot = self.foot
        for k in range(ps.shape[0]):
            self.own[k * DK : (k + 1) * DK, :] = ps[k].astype(bf16)
        self.own[foot:, :DK] = jnp.full((16, DK), first_doc.astype(f32)).astype(bf16)
        self.own[foot:, DK:] = jnp.full((16, DK), last_doc.astype(f32)).astype(bf16)
        for copy in self.first_round():
            copy.start()

    def again(self):
        for copy in self.first_round():
            copy.wait()
        foot, own, near, s = self.foot, self.own, self.near, self.me.s
        first_own, last_one = own[foot : foot + 1, 0:1], near[0, foot : foot + 1, DK : DK + 1]
        first_one, last_two = near[0, foot : foot + 1, 0:1], near[1, foot : foot + 1, DK : DK + 1]
        for k in range(foot // DK):
            rows = slice(k * DK, (k + 1) * DK)
            two = join(near[1, rows, :], near[0, rows, :], (last_two == first_one) & (s >= 2))
            self.three[rows, :] = join(two, own[rows, :], (last_one == first_own) & (s >= 1))
        self.three[foot:, :DK] = near[1, foot:, :DK]
        self.three[foot:, DK:] = own[foot:, DK:]
        for copy in self.second_round():
            copy.start()

    def entering(self):
        for copy in self.second_round():
            copy.wait()
        foot, far1, far4, s = self.foot, self.far1, self.far4, self.me.s
        first_own, last_one = self.own[foot : foot + 1, 0:1], far1[foot : foot + 1, DK : DK + 1]
        first_three, last_four = far1[foot : foot + 1, 0:1], far4[foot : foot + 1, 0:1]
        states = []
        for k in range(foot // DK):
            rows = slice(k * DK, (k + 1) * DK)
            older = jnp.where(
                (last_four == first_three) & (s >= 4), dot(far1[rows, :DK], far4[rows, :]), 0.0
            )
            state = older + far1[rows, DK:].astype(f32)
            states.append(jnp.where((last_one == first_own) & (s >= 1), state, 0.0).astype(bf16))
        return states


class Mixer:
    def __init__(self, me, normed, gath, w, obuf, result, there_s, there_r, share_s, share_r, back_s, back_r):
        self.me, self.normed, self.gath, self.w = me, normed, gath, w
        self.obuf, self.result = obuf, result
        self.there_s, self.there_r, self.share_s, self.share_r = there_s, there_r, share_s, share_r
        self.back_s, self.back_r = back_s, back_r
        self.width = normed.shape[1]
        self.part = normed.shape[0] // me.chips
        self.sub = self.part // SUBS

    def rows(self, d, r):
        chip_at = lax.rem(self.me.y + d + self.me.chips, self.me.chips)
        return pl.ds(pl.multiple_of(chip_at * self.part + r * self.sub, self.sub), self.sub)

    def spot(self, r, d, core):
        block = (self.me.chips - d) % self.me.chips * 2 + core
        lanes = pl.ds(pl.multiple_of(block * self.width, self.width), self.width)
        return self.gath.at[r * self.sub : (r + 1) * self.sub, lanes]

    def there(self, r, d):
        return pltpu.make_async_remote_copy(
            src_ref=self.normed.at[self.rows(d, r), :],
            dst_ref=self.spot(r, d, self.me.c),
            send_sem=self.there_s.at[r, d],
            recv_sem=self.there_r.at[r, d],
            **self.me.chip(d, self.me.c),
        )

    def share(self, r, d):
        at = self.spot(r, d, self.me.c)
        return pltpu.make_async_remote_copy(
            src_ref=self.normed.at[self.rows(0, r), :] if d == 0 else at,
            dst_ref=at,
            send_sem=self.share_s.at[r, d],
            recv_sem=self.share_r.at[r, d],
            **self.me.beside(),
        )

    def back(self, r, t, e):
        return pltpu.make_async_remote_copy(
            src_ref=self.obuf.at[r, t],
            dst_ref=self.result.at[self.rows(0, r), :],
            send_sem=self.back_s.at[r, t],
            recv_sem=self.back_r.at[r, e],
            **peer(self.me.s, 2 * self.me.chips // 2 * self.me.c + t),
        )

    def home(self, r, t):
        return pltpu.make_async_copy(
            self.obuf.at[r, t], self.result.at[self.rows(0, r), :], self.back_s.at[r, t]
        )

    def target(self, t):
        at = self.me.chips * self.me.c + t
        far = lax.rem(at // 2 - self.me.y + self.me.chips, self.me.chips)
        return far, at == self.me.y * 2 + self.me.c

    def run(self):
        me, chips = self.me, self.me.chips
        order = [2, 1, 3]
        for r in range(SUBS):
            self.share(r, 0).start()
            self.spot(r, 0, me.c)[...] = self.normed[self.rows(0, r), :]
        for r in range(SUBS):
            for d in [1, 3, 2]:
                self.there(r, d).wait_recv()
                self.share(r, d).start()
            for d in range(chips):
                self.share(r, d).wait_recv()
            block = self.gath[r * self.sub : (r + 1) * self.sub, :]
            w = self.w[...].reshape(self.w.shape[0] * self.w.shape[1], self.w.shape[2])
            for t in range(chips):
                cut = w[:, t * self.width : (t + 1) * self.width]
                self.obuf[r, t] = dot(block, cut).astype(bf16)
                far, mine = self.target(t)

                @pl.when(jnp.logical_not(mine))
                def _():
                    self.back(r, t, far).start()

                @pl.when(mine)
                def _():
                    self.home(r, t).start()

        for r in range(SUBS):
            for d in order:
                self.there(r, d).wait_send()
            for d in range(chips):
                self.share(r, d).wait_send()
            for t in range(chips):
                far, mine = self.target(t)

                @pl.when(jnp.logical_not(mine))
                def _():
                    self.back(r, t, far).wait_send()

                @pl.when(mine)
                def _():
                    self.home(r, t).wait()

            for e in range(1, chips):
                self.back(r, 0, e).wait_recv()

            @pl.when(me.c != me.y // (chips // 2))
            def _():
                self.back(r, 0, 0).wait_recv()


def layer_kernel(
    doc, x, gain, wk, wv, wb, wq, out_gain, wo, result,
    weights, wqs, keys, vbuf, bbuf, scale, wu, ps_all, ps, strict, causal, pair, off,
    out, carried, own, near, three, far1, far4, normed, gath, w, obuf,
    over_s, over_r, near_s, ring_s, ring_r, st_s, st_r,
    there_s, there_r, share_s, share_r, back_s, back_r,
):
    i = pl.program_id(0)
    tile, count = x.shape[0], doc.shape[0]
    blocks = tile // BLOCK
    tiles = count // blocks
    me = Place()
    gather = WeightGather(me, wo, w, over_s, over_r, near_s, ring_s, ring_r)
    states = StateExchange(me, own, near, three, far1, far4, st_s, st_r)
    mixer = Mixer(
        me, normed, gath, w, obuf, result, there_s, there_r, share_s, share_r, back_s, back_r
    )

    def at_tile(j):
        return pl.ds(pl.multiple_of(j * tile, tile), tile)

    def project():
        at = at_tile(jnp.minimum(i, tiles - 1))
        return project_keys(x, scale.at[at, :], weights, keys.at[:, at, :], vbuf, bbuf, i % 2)

    def solve():
        j = jnp.clip(i - 1, 0, tiles - 1)
        at = at_tile(j)
        chunks = pl.ds(pl.multiple_of(j * (tile // DK), tile // DK), tile // DK)
        return solve_keys(
            doc, j * blocks, keys.at[:, at, :], vbuf, bbuf, (i + 1) % 2, ps,
            (strict, pair, off), wu.at[:, at, :], ps_all.at[:, chunks],
        )

    @pl.when(i == 0)
    def _():
        barrier = pltpu.get_barrier_semaphore()
        for at in me.peers():
            pl.semaphore_signal(barrier, inc=1, **at)
        fill_masks(strict, causal, pair, off)
        sk, sv = scaled_weight(wk, gain), scaled_weight(wv, gain)
        for h in range(2):
            weights[:, 2 * h * DK : (2 * h + 1) * DK] = sk[:, h * DK : (h + 1) * DK]
            weights[:, (2 * h + 1) * DK : (2 * h + 2) * DK] = sv[:, h * DK : (h + 1) * DK]
        rest = jnp.zeros((DK - wb.shape[0], wb.shape[1]), f32)
        padded = jnp.concatenate([wb[...].astype(f32) * gain[...], rest], axis=0)
        weights[:, 4 * DK :] = jnp.transpose(padded).astype(bf16)
        pl.semaphore_wait(barrier, len(me.peers()))
        gather.begin()
        row = lax.broadcasted_iota(jnp.int32, (DK, 2 * DK), 0)
        col = lax.broadcasted_iota(jnp.int32, (DK, 2 * DK), 1)
        for h in range(2):
            ps[h] = jnp.where(row == col, 1.0, 0.0).astype(f32)
        for _ in project():
            pass

    @pl.when(i == SPREAD_AT)
    def _():
        gather.spread()

    @pl.when((i > 0) & (i < tiles))
    def _():
        interleave(solve(), project(), 2)

    @pl.when(i == tiles)
    def _():
        for _ in solve():
            pass
        states.begin(ps, doc[0], doc[count - 1])
        wqs[...] = scaled_weight(wq, gain)

    @pl.when(i == 2 * tiles)
    def _():
        states.again()

    @pl.when(i > tiles)
    def _():
        j = jnp.clip(i - tiles - 1, 0, tiles - 1)
        at = at_tile(j)
        chunks = pl.ds(pl.multiple_of(j * (tile // DK), tile // DK), tile // DK)
        query_tile(
            doc, j * blocks, x, scale.at[at, :], wqs, keys.at[:, at, :], wu.at[:, at, :],
            ps_all.at[:, chunks], causal, out.at[:, at, :], carried.at[:, at, :],
        )

    @pl.when(i == 2 * tiles)
    def _():
        entering = states.entering()
        for r in range(SUBS):
            for d in (2, 1, 3, 0):
                rows = mixer.rows(d, r)
                for k in range(len(entering)):
                    o = out[k, rows, :] + dot(carried[k, rows, :], entering[k])
                    size = lax.rsqrt(jnp.mean(o * o, axis=1, keepdims=True) + norm_eps)
                    normed[rows, k * DK : (k + 1) * DK] = (o * size * out_gain[...]).astype(bf16)
                if d:
                    mixer.there(r, d).start()
        gather.finish()
        mixer.run()


def layer_pass(doc, tokens, gain, wk, wv, wb, wq, out_gain, wo):
    length, width = tokens.shape
    heads = wb.shape[0]
    tiles = length // TILE
    depth = wo.shape[0]
    chips = wo.shape[1] // depth // 2
    part = length // chips
    sub = part // SUBS
    message = (heads * DK + 16, 2 * DK)
    dma = lambda *shape: pltpu.SemaphoreType.DMA(shape)
    whole = lambda shape: pl.BlockSpec(
        shape, lambda i, doc: (0,) * len(shape), pipeline_mode=pl.Buffered(1)
    )
    return pl.pallas_call(
        layer_kernel,
        grid_spec=pltpu.PrefetchScalarGridSpec(
            num_scalar_prefetch=1,
            grid=(2 * tiles + 1,),
            in_specs=[
                pl.BlockSpec(
                    (TILE, width),
                    lambda i, doc: (
                        jnp.where(i > tiles, i - tiles - 1, jnp.minimum(i, tiles - 1)),
                        0,
                    ),
                ),
                whole((1, width)),
                whole(wk.shape),
                whole(wv.shape),
                whole(wb.shape),
                whole(wq.shape),
                whole(out_gain.shape),
                pl.BlockSpec(memory_space=pl.ANY),
            ],
            out_specs=pl.BlockSpec(memory_space=pl.ANY),
            scratch_shapes=[
                pltpu.VMEM((width, 5 * DK), bf16),
                pltpu.VMEM(wq.shape, bf16),
                pltpu.VMEM((heads, length, DK), bf16),
                pltpu.VMEM((2, heads, TILE, DK), f32),
                pltpu.VMEM((2, TILE, DK), f32),
                pltpu.VMEM((length, DK), f32),
                pltpu.VMEM((heads, length, 2 * DK), bf16),
                pltpu.VMEM((heads, length // DK, DK, 2 * DK), bf16),
                pltpu.VMEM((heads, DK, 2 * DK), f32),
                pltpu.VMEM((STEP, STEP), f32),
                pltpu.VMEM((STEP, STEP), f32),
                pltpu.VMEM((2, STEP, STEP), bf16),
                pltpu.VMEM((len(LEVELS), STEP, STEP), bf16),
                pltpu.VMEM((heads, length, DK), f32),
                pltpu.VMEM((heads, length, DK), bf16),
                pltpu.VMEM(message, bf16),
                pltpu.VMEM((2,) + message, bf16),
                pltpu.VMEM(message, bf16),
                pltpu.VMEM(message, bf16),
                pltpu.VMEM((message[0], DK), bf16),
                pltpu.VMEM((length, heads * DK), bf16),
                pltpu.VMEM((part, wo.shape[1]), bf16),
                pltpu.VMEM((2 * chips, depth, wo.shape[1] // 2), bf16),
                pltpu.VMEM((SUBS, chips, sub, depth), bf16),
                dma(chips - 1, 2, 2),
                dma(chips - 1, 2, 2),
                dma(3),
                dma(2, SIDE - 1),
                dma(2, SIDE - 1),
                dma(4),
                dma(4),
            ]
            + [dma(SUBS, chips)] * 6,
        ),
        out_shape=jax.ShapeDtypeStruct((length, heads * DK), bf16),
        compiler_params=pltpu.CompilerParams(
            vmem_limit_bytes=58 << 20, collective_id=0, has_side_effects=True
        ),
        name="layer_pass",
    )(doc, tokens, gain, wk, wv, wb, wq, out_gain, wo)


def local(tokens, norm_gain, wq, wk, wv, wb, out_gain, wo, block_doc):
    return layer_pass(
        block_doc, tokens, norm_gain[None, :], wk, wv, wb.T, wq, out_gain[None, :], wo
    )


def solution(mesh):
    in_specs = (
        P("seq", None),
        P(),
        P(None, "head"),
        P(None, "head"),
        P(None, "head"),
        P(None, "head"),
        P(),
        P("head", None),
        P("seq"),
    )
    return jax.shard_map(
        local, mesh=mesh, in_specs=in_specs, out_specs=P("seq", "head"), check_vma=False
    )
```

```python
import jax
import jax.numpy as jnp
from jax import lax
from jax.experimental import pallas as pl
from jax.experimental.pallas import tpu as pltpu
from jax.sharding import PartitionSpec as P

norm_eps = 1e-05
key_eps = 1e-06
BLOCK = 64
DK = 128
STEP = 256
TILE = 512
SIDE = 4
SPREAD_AT = 2
RINGED = 1
SUBS = 4
f32 = jnp.float32
bf16 = jnp.bfloat16
LEVELS = (2, 4, 8, 16, 32, 64)


def dot(a, b):
    return jnp.dot(a, b, preferred_element_type=f32)


def dot_nt(a, b):
    return lax.dot_general(a, b, (((1,), (1,)), ((), ())), preferred_element_type=f32)


def dot_tn(a, b):
    return lax.dot_general(a, b, (((0,), (0,)), ((), ())), preferred_element_type=f32)


def unit(values):
    act = values * jax.nn.sigmoid(values)
    return act * lax.rsqrt(jnp.sum(act * act, axis=1, keepdims=True) + key_eps)


def peer(s, h):
    return dict(device_id=(s, h), device_id_type=pl.DeviceIdType.MESH)


def fill_masks(strict, causal, pair, off):
    shape = (STEP, STEP)
    row = lax.broadcasted_iota(jnp.int32, shape, 0)
    col = lax.broadcasted_iota(jnp.int32, shape, 1)
    same = (row // DK) == (col // DK)
    strict[...] = jnp.where(same & (row > col), 1.0, 0.0).astype(f32)
    causal[...] = jnp.where(same & (row >= col), 1.0, 0.0).astype(f32)
    pair[0] = jnp.where((row // 2 == col // 2) & (row > col), 1.0, 0.0).astype(bf16)
    pair[1] = jnp.where(row == col, 1.0, 0.0).astype(bf16)
    for n, s in enumerate(LEVELS):
        hit = (row // (2 * s) == col // (2 * s)) & (row // s > col // s)
        off[n] = jnp.where(hit, 1.0, 0.0).astype(bf16)


def scaled_weight(weight, gain):
    column = jnp.transpose(jnp.broadcast_to(gain[...], (DK, gain.shape[1])))
    parts = [
        weight[:, n * DK : (n + 1) * DK].astype(f32) * column for n in range(weight.shape[1] // DK)
    ]
    return jnp.concatenate(parts, axis=1).astype(bf16)


def doc_masks(doc, at):
    d = [doc[at + j] for j in range(4)]
    before = doc[jnp.maximum(at - 1, 0)]
    link = [
        jnp.where((before == d[0]) | (at == 0), 1.0, 0.0).astype(f32),
        jnp.where(d[1] == d[2], 1.0, 0.0).astype(f32),
    ]
    join = [
        jnp.where(d[0] == d[1], 1.0, 0.0).astype(f32),
        jnp.where(d[2] == d[3], 1.0, 0.0).astype(f32),
    ]
    row = lax.broadcasted_iota(jnp.int32, (STEP, 1), 0)
    second = (row % DK) >= BLOCK
    join_r = jnp.where(row >= DK, join[1], join[0])
    link_r = jnp.where(row >= DK, link[1], link[0])
    enters = jnp.where(second, link_r * join_r, link_r)
    leaves = jnp.where(second, 1.0, join_r)
    cross = jnp.where(second, join_r, 1.0)
    col = lax.broadcasted_iota(jnp.int32, (1, STEP), 1)
    full = jnp.where((col % DK) < BLOCK, cross, 1.0)
    return enters, leaves, full, [link[c] * join[c] for c in range(2)]


def upper(a, size):
    return jnp.concatenate([a[j : j + size] for j in range(0, a.shape[0], 2 * size)], axis=0)


def lower(a, size):
    return jnp.concatenate([a[j + size : j + 2 * size] for j in range(0, a.shape[0], 2 * size)], axis=0)


def spread_rows(first, second, size):
    parts = []
    for j in range(0, first.shape[0], size):
        parts += [first[j : j + size], second[j : j + size]]
    return jnp.concatenate(parts, axis=0)


def interleave(main, side, every):
    count = 0
    for _ in main:
        count += 1
        if count % every == 0:
            next(side, None)
    for _ in side:
        pass


def project_keys(x, scale_out, weights, keys_at, vbuf, bbuf, slot):
    halves = x.shape[0] // STEP
    scales = []
    for m in range(halves):
        rows = slice(m * STEP, (m + 1) * STEP)
        floats = x[rows, :].astype(f32)
        r = lax.rsqrt(jnp.mean(floats * floats, axis=1, keepdims=True) + norm_eps)
        scales.append(r)
        scale_out[rows, :] = jnp.broadcast_to(r, (STEP, DK))
        yield
        b = dot(x[rows, :], weights[:, 4 * DK :]) * r
        bbuf[slot, rows, :] = jax.nn.sigmoid(b)
        yield
        for h in range(2):
            kv = dot(x[rows, :], weights[:, 2 * h * DK : 2 * (h + 1) * DK]) * r
            keys_at[h, rows, :] = unit(kv[:, :DK]).astype(bf16)
            vbuf[slot, h, rows, :] = kv[:, DK:]
            yield


def solve_keys(doc, at, keys_at, vbuf, bbuf, slot, ps, masks, wu_out, ps_all):
    strict, pair, off = masks
    halves = keys_at.shape[1] // STEP
    groups = [(h, g) for g in range(halves) for h in range(2)]
    dm = [doc_masks(doc, at + 4 * g) for g in range(halves)]
    keys, a_hi, a_lo, xb, t, right, y, wu = {}, {}, {}, {}, {}, {}, {}, {}
    beta = {}
    for h, g in groups:
        rows = slice(g * STEP, (g + 1) * STEP)
        keys[h, g] = keys_at[h, rows, :]
        beta[h, g] = bbuf[slot, rows, h : h + 1]
        a = dot_nt(keys[h, g], keys[h, g]) * beta[h, g] * (strict[...] * dm[g][2])
        hi = a.astype(bf16)
        a_hi[h, g] = hi
        a_lo[h, g] = (a - hi.astype(f32)).astype(bf16)
        xb[h, g] = pair[1] - hi * pair[0]
        yield
    for n, size in enumerate(LEVELS):
        if size < 16:
            for k in groups:
                t[k] = dot(a_hi[k] * off[n], xb[k]).astype(bf16)
            yield
            for k in groups:
                xb[k] = xb[k] - dot(xb[k], t[k]).astype(bf16)
            yield
            continue
        for k in groups:
            low = dot(lower(a_hi[k], size) * lower(off[n], size), xb[k]).astype(bf16)
            t[k] = spread_rows(jnp.zeros_like(low), low, size)
        yield
        for k in groups:
            low = lower(xb[k], size)
            low = low - dot(low, t[k]).astype(bf16)
            xb[k] = spread_rows(upper(xb[k], size), low, size)
        yield
    for h, g in groups:
        rows = slice(g * STEP, (g + 1) * STEP)
        b = beta[h, g]
        right[h, g] = jnp.concatenate(
            [(b * dm[g][0]) * keys[h, g].astype(f32), b * vbuf[slot, h, rows, :]], axis=1
        )
        y[h, g] = dot(xb[h, g], right[h, g].astype(bf16)).astype(bf16)
    yield
    left = {}
    for k in groups:
        rest = right[k] - y[k].astype(f32) - dot(a_hi[k], y[k]) - dot(a_lo[k], y[k])
        left[k] = rest.astype(bf16)
    yield
    for h, g in groups:
        wu[h, g] = (y[h, g].astype(f32) + dot(xb[h, g], left[h, g])).astype(bf16)
        wu_out[h, g * STEP : (g + 1) * STEP, :] = wu[h, g]
    yield
    step = {}
    for h, g in groups:
        k_end = (keys[h, g].astype(f32) * dm[g][1]).astype(bf16)
        for c in range(2):
            rows = slice(c * DK, (c + 1) * DK)
            step[h, g, c] = dot_tn(k_end[rows], wu[h, g][rows])
    yield
    for g in range(halves):
        for c in range(2):
            for h in range(2):
                state = ps[h]
                sb = state.astype(bf16)
                ps_all[h, 2 * g + c] = sb
                move = step[h, g, c]
                moved = dot(move[:, :DK].astype(bf16), sb)
                gain = jnp.concatenate([jnp.zeros((DK, DK), f32), move[:, DK:]], axis=1)
                ps[h] = dm[g][3][c] * state - moved + gain
            yield


def query_tile(doc, at, x, scale, weights, keys, wu, ps_all, causal, out, carried):
    groups = [(h, g) for g in range(x.shape[0] // STEP) for h in range(2)]
    dm = [doc_masks(doc, at + 4 * g) for g in range(x.shape[0] // STEP)]
    qb, mixed, scores = {}, {}, {}
    for g in range(x.shape[0] // STEP):
        rows = slice(g * STEP, (g + 1) * STEP)
        both = dot(x[rows, :], weights[...]) * scale[rows, 0:1]
        for h in range(2):
            qb[h, g] = unit(both[:, h * DK : (h + 1) * DK]).astype(bf16)
    for h, g in groups:
        rows = slice(g * STEP, (g + 1) * STEP)
        s = dot_nt(qb[h, g], keys[h, rows, :]) * (causal[...] * dm[g][2])
        scores[h, g] = s.astype(bf16)
    for h, g in groups:
        rows = slice(g * STEP, (g + 1) * STEP)
        mixed[h, g] = dot(scores[h, g], wu[h, rows, :])
    for h, g in groups:
        reach = (dm[g][0] * qb[h, g].astype(f32) - mixed[h, g][:, :DK]).astype(bf16)
        for c in range(2):
            rows = slice(c * DK, (c + 1) * DK)
            to = slice(g * STEP + c * DK, g * STEP + (c + 1) * DK)
            seen = dot(reach[rows], ps_all[h, 2 * g + c])
            carried[h, to, :] = seen[:, :DK].astype(bf16)
            out[h, to, :] = mixed[h, g][rows, DK:] + seen[:, DK:]


class Place:
    def __init__(self):
        self.s, h = lax.axis_index("seq"), lax.axis_index("head")
        self.length = lax.axis_size("seq")
        self.chips = lax.axis_size("head") // 2
        self.y, self.c = h // 2, lax.rem(h, 2)
        self.outer, self.inner = self.s // SIDE, lax.rem(self.s, SIDE)

    def later(self, d):
        return peer(lax.rem(self.s + d + self.length, self.length), self.y * 2 + self.c)

    def chip(self, d, core):
        return peer(self.s, lax.rem(self.y + d + self.chips, self.chips) * 2 + core)

    def beside(self):
        return self.chip(0, 1 - self.c)

    def along(self, axis, d):
        if axis == 0:
            s = lax.rem(self.outer + d + SIDE, SIDE) * SIDE + self.inner
        else:
            s = self.outer * SIDE + lax.rem(self.inner + d + SIDE, SIDE)
        return peer(s, self.y * 2 + self.c)

    def peers(self):
        found = [self.chip(d, core) for d in range(1, self.chips) for core in range(2)]
        found.append(self.beside())
        found += [self.along(a, d) for a in range(2) for d in range(1, SIDE)]
        return found + [self.later(d) for d in (1, -1, 2, -2, 4, -4)]


class WeightGather:
    def __init__(self, me, wo, w, over_s, over_r, near_s, ring_s, ring_r):
        self.me, self.wo, self.w = me, wo, w
        self.over_s, self.over_r, self.near_s = over_s, over_r, near_s
        self.ring_s, self.ring_r = ring_s, ring_r
        self.depth, self.half = w.shape[1], w.shape[2]
        self.quarter, self.wide = self.depth // SIDE, self.half // 2

    def rows(self, axis):
        q = self.me.outer if axis == 0 else self.me.inner
        return pl.ds(pl.multiple_of(q * self.quarter, self.quarter), self.quarter)

    def over(self, d, core, axis, origin):
        start = core * self.half + axis * self.wide
        block = (self.me.chips - d) * 2 + origin
        rows = self.rows(axis) if axis < RINGED else slice(None)
        return pltpu.make_async_remote_copy(
            src_ref=self.wo.at[rows, start : start + self.wide],
            dst_ref=self.w.at[block, rows, axis * self.wide : (axis + 1) * self.wide],
            send_sem=self.over_s.at[d - 1, core, axis],
            recv_sem=self.over_r.at[d - 1, origin, axis],
            **self.me.chip(d, core),
        )

    def columns(self, core):
        return pl.ds(pl.multiple_of(core * self.half, self.half), self.half)

    def pair(self):
        return pltpu.make_async_remote_copy(
            src_ref=self.wo.at[:, self.columns(1 - self.me.c)],
            dst_ref=self.w.at[self.me.c],
            send_sem=self.near_s.at[0],
            recv_sem=self.near_s.at[1],
            **self.me.beside(),
        )

    def own(self):
        return pltpu.make_async_copy(
            self.wo.at[:, self.columns(self.me.c)], self.w.at[self.me.c], self.near_s.at[2]
        )

    def ring(self, axis, d):
        at = self.w.at[2:, self.rows(axis), axis * self.wide : (axis + 1) * self.wide]
        return pltpu.make_async_remote_copy(
            src_ref=at,
            dst_ref=at,
            send_sem=self.ring_s.at[axis, d - 1],
            recv_sem=self.ring_r.at[axis, d - 1],
            **self.me.along(axis, d),
        )

    def each_over(self):
        return [(d, k, a) for a in range(2) for d in (2, 1, 3) for k in range(2)]

    def each_ring(self):
        return [(a, d) for d in (2, 1, 3) for a in range(RINGED)]

    def begin(self):
        for d, core, axis in self.each_over():
            self.over(d, core, axis, self.me.c).start()
        self.pair().start()
        self.own().start()

    def spread(self):
        for d, core, axis in self.each_over():
            if axis < RINGED:
                self.over(d, core, axis, core).wait_recv()
        for at in self.each_ring():
            self.ring(*at).start()

    def finish(self):
        for d, core, axis in self.each_over():
            self.over(d, core, axis, self.me.c).wait_send()
            if axis >= RINGED:
                self.over(d, core, axis, core).wait_recv()
        self.pair().wait()
        self.own().wait()
        for at in self.each_ring():
            self.ring(*at).wait()


def join(first, then, follows):
    moved = jnp.where(follows, dot(then[:, :DK], first), 0.0)
    gain = jnp.concatenate([jnp.zeros((DK, DK), f32), then[:, DK:].astype(f32)], axis=1)
    return (moved + gain).astype(bf16)


class StateExchange:
    def __init__(self, me, own, near, three, far1, far4, send, recv):
        self.me = me
        self.own, self.near, self.three, self.far1, self.far4 = own, near, three, far1, far4
        self.send, self.recv = send, recv
        self.foot = own.shape[0] - 16

    def move(self, src, dst, at, d):
        return pltpu.make_async_remote_copy(
            src_ref=src, dst_ref=dst, send_sem=self.send.at[at], recv_sem=self.recv.at[at],
            **self.me.later(d),
        )

    def first_round(self):
        return [self.move(self.own, self.near.at[0], 0, 1), self.move(self.own, self.near.at[1], 1, 2)]

    def second_round(self):
        return [
            self.move(self.three, self.far1, 2, 1),
            self.move(self.three.at[:, DK:], self.far4, 3, 4),
        ]

    def begin(self, ps, first_doc, last_doc):
        foot = self.foot
        for k in range(ps.shape[0]):
            self.own[k * DK : (k + 1) * DK, :] = ps[k].astype(bf16)
        self.own[foot:, :DK] = jnp.full((16, DK), first_doc.astype(f32)).astype(bf16)
        self.own[foot:, DK:] = jnp.full((16, DK), last_doc.astype(f32)).astype(bf16)
        for copy in self.first_round():
            copy.start()

    def again(self):
        for copy in self.first_round():
            copy.wait()
        foot, own, near, s = self.foot, self.own, self.near, self.me.s
        first_own, last_one = own[foot : foot + 1, 0:1], near[0, foot : foot + 1, DK : DK + 1]
        first_one, last_two = near[0, foot : foot + 1, 0:1], near[1, foot : foot + 1, DK : DK + 1]
        for k in range(foot // DK):
            rows = slice(k * DK, (k + 1) * DK)
            two = join(near[1, rows, :], near[0, rows, :], (last_two == first_one) & (s >= 2))
            self.three[rows, :] = join(two, own[rows, :], (last_one == first_own) & (s >= 1))
        self.three[foot:, :DK] = near[1, foot:, :DK]
        self.three[foot:, DK:] = own[foot:, DK:]
        for copy in self.second_round():
            copy.start()

    def entering(self):
        for copy in self.second_round():
            copy.wait()
        foot, far1, far4, s = self.foot, self.far1, self.far4, self.me.s
        first_own, last_one = self.own[foot : foot + 1, 0:1], far1[foot : foot + 1, DK : DK + 1]
        first_three, last_four = far1[foot : foot + 1, 0:1], far4[foot : foot + 1, 0:1]
        states = []
        for k in range(foot // DK):
            rows = slice(k * DK, (k + 1) * DK)
            older = jnp.where(
                (last_four == first_three) & (s >= 4), dot(far1[rows, :DK], far4[rows, :]), 0.0
            )
            state = older + far1[rows, DK:].astype(f32)
            states.append(jnp.where((last_one == first_own) & (s >= 1), state, 0.0).astype(bf16))
        return states


class Mixer:
    def __init__(self, me, normed, gath, w, obuf, result, there_s, there_r, share_s, share_r, back_s, back_r):
        self.me, self.normed, self.gath, self.w = me, normed, gath, w
        self.obuf, self.result = obuf, result
        self.there_s, self.there_r, self.share_s, self.share_r = there_s, there_r, share_s, share_r
        self.back_s, self.back_r = back_s, back_r
        self.width = normed.shape[1]
        self.part = normed.shape[0] // me.chips
        self.sub = self.part // SUBS

    def rows(self, d, r):
        chip_at = lax.rem(self.me.y + d + self.me.chips, self.me.chips)
        return pl.ds(pl.multiple_of(chip_at * self.part + r * self.sub, self.sub), self.sub)

    def spot(self, r, d, core):
        block = (self.me.chips - d) % self.me.chips * 2 + core
        lanes = pl.ds(pl.multiple_of(block * self.width, self.width), self.width)
        return self.gath.at[r * self.sub : (r + 1) * self.sub, lanes]

    def there(self, r, d):
        return pltpu.make_async_remote_copy(
            src_ref=self.normed.at[self.rows(d, r), :],
            dst_ref=self.spot(r, d, self.me.c),
            send_sem=self.there_s.at[r, d],
            recv_sem=self.there_r.at[r, d],
            **self.me.chip(d, self.me.c),
        )

    def share(self, r, d):
        at = self.spot(r, d, self.me.c)
        return pltpu.make_async_remote_copy(
            src_ref=self.normed.at[self.rows(0, r), :] if d == 0 else at,
            dst_ref=at,
            send_sem=self.share_s.at[r, d],
            recv_sem=self.share_r.at[r, d],
            **self.me.beside(),
        )

    def back(self, r, t, e):
        return pltpu.make_async_remote_copy(
            src_ref=self.obuf.at[r, t],
            dst_ref=self.result.at[self.rows(0, r), :],
            send_sem=self.back_s.at[r, t],
            recv_sem=self.back_r.at[r, e],
            **peer(self.me.s, 2 * self.me.chips // 2 * self.me.c + t),
        )

    def home(self, r, t):
        return pltpu.make_async_copy(
            self.obuf.at[r, t], self.result.at[self.rows(0, r), :], self.back_s.at[r, t]
        )

    def target(self, t):
        at = self.me.chips * self.me.c + t
        far = lax.rem(at // 2 - self.me.y + self.me.chips, self.me.chips)
        return far, at == self.me.y * 2 + self.me.c

    def run(self, weight_here):
        me, chips = self.me, self.me.chips
        order = [2, 1, 3]
        for r in range(SUBS):
            self.share(r, 0).start()
            self.spot(r, 0, me.c)[...] = self.normed[self.rows(0, r), :]
        for r in range(SUBS):
            for d in [1, 3, 2]:
                self.there(r, d).wait_recv()
                self.share(r, d).start()
            for d in range(chips):
                self.share(r, d).wait_recv()
            if r == 0:
                weight_here()
            block = self.gath[r * self.sub : (r + 1) * self.sub, :]
            w = self.w[...].reshape(self.w.shape[0] * self.w.shape[1], self.w.shape[2])
            for t in range(chips):
                cut = w[:, t * self.width : (t + 1) * self.width]
                self.obuf[r, t] = dot(block, cut).astype(bf16)
                far, mine = self.target(t)

                @pl.when(jnp.logical_not(mine))
                def _():
                    self.back(r, t, far).start()

                @pl.when(mine)
                def _():
                    self.home(r, t).start()

        for r in range(SUBS):
            for d in order:
                self.there(r, d).wait_send()
            for d in range(chips):
                self.share(r, d).wait_send()
            for t in range(chips):
                far, mine = self.target(t)

                @pl.when(jnp.logical_not(mine))
                def _():
                    self.back(r, t, far).wait_send()

                @pl.when(mine)
                def _():
                    self.home(r, t).wait()

            for e in range(1, chips):
                self.back(r, 0, e).wait_recv()

            @pl.when(me.c != me.y // (chips // 2))
            def _():
                self.back(r, 0, 0).wait_recv()


def layer_kernel(
    doc, x, gain, wk, wv, wb, wq, out_gain, wo, result,
    weights, wqs, keys, vbuf, bbuf, scale, wu, ps_all, ps, strict, causal, pair, off,
    out, carried, own, near, three, far1, far4, normed, gath, w, obuf,
    over_s, over_r, near_s, ring_s, ring_r, st_s, st_r,
    there_s, there_r, share_s, share_r, back_s, back_r,
):
    i = pl.program_id(0)
    tile, count = x.shape[0], doc.shape[0]
    blocks = tile // BLOCK
    tiles = count // blocks
    me = Place()
    gather = WeightGather(me, wo, w, over_s, over_r, near_s, ring_s, ring_r)
    states = StateExchange(me, own, near, three, far1, far4, st_s, st_r)
    mixer = Mixer(
        me, normed, gath, w, obuf, result, there_s, there_r, share_s, share_r, back_s, back_r
    )

    def at_tile(j):
        return pl.ds(pl.multiple_of(j * tile, tile), tile)

    def project():
        at = at_tile(jnp.minimum(i, tiles - 1))
        return project_keys(x, scale.at[at, :], weights, keys.at[:, at, :], vbuf, bbuf, i % 2)

    def solve():
        j = jnp.clip(i - 1, 0, tiles - 1)
        at = at_tile(j)
        chunks = pl.ds(pl.multiple_of(j * (tile // DK), tile // DK), tile // DK)
        return solve_keys(
            doc, j * blocks, keys.at[:, at, :], vbuf, bbuf, (i + 1) % 2, ps,
            (strict, pair, off), wu.at[:, at, :], ps_all.at[:, chunks],
        )

    @pl.when(i == 0)
    def _():
        barrier = pltpu.get_barrier_semaphore()
        for at in me.peers():
            pl.semaphore_signal(barrier, inc=1, **at)
        fill_masks(strict, causal, pair, off)
        sk, sv = scaled_weight(wk, gain), scaled_weight(wv, gain)
        for h in range(2):
            weights[:, 2 * h * DK : (2 * h + 1) * DK] = sk[:, h * DK : (h + 1) * DK]
            weights[:, (2 * h + 1) * DK : (2 * h + 2) * DK] = sv[:, h * DK : (h + 1) * DK]
        rest = jnp.zeros((DK - wb.shape[0], wb.shape[1]), f32)
        padded = jnp.concatenate([wb[...].astype(f32) * gain[...], rest], axis=0)
        weights[:, 4 * DK :] = jnp.transpose(padded).astype(bf16)
        pl.semaphore_wait(barrier, len(me.peers()))
        gather.begin()
        row = lax.broadcasted_iota(jnp.int32, (DK, 2 * DK), 0)
        col = lax.broadcasted_iota(jnp.int32, (DK, 2 * DK), 1)
        for h in range(2):
            ps[h] = jnp.where(row == col, 1.0, 0.0).astype(f32)
        for _ in project():
            pass

    @pl.when(i == SPREAD_AT)
    def _():
        gather.spread()

    @pl.when((i > 0) & (i < tiles))
    def _():
        interleave(solve(), project(), 2)

    @pl.when(i == tiles)
    def _():
        for _ in solve():
            pass
        states.begin(ps, doc[0], doc[count - 1])
        wqs[...] = scaled_weight(wq, gain)

    @pl.when(i == 2 * tiles)
    def _():
        states.again()

    @pl.when(i > tiles)
    def _():
        j = jnp.clip(i - tiles - 1, 0, tiles - 1)
        at = at_tile(j)
        chunks = pl.ds(pl.multiple_of(j * (tile // DK), tile // DK), tile // DK)
        query_tile(
            doc, j * blocks, x, scale.at[at, :], wqs, keys.at[:, at, :], wu.at[:, at, :],
            ps_all.at[:, chunks], causal, out.at[:, at, :], carried.at[:, at, :],
        )

    @pl.when(i == 2 * tiles)
    def _():
        entering = states.entering()
        for r in range(SUBS):
            for d in (2, 1, 3, 0):
                rows = mixer.rows(d, r)
                for k in range(len(entering)):
                    o = out[k, rows, :] + dot(carried[k, rows, :], entering[k])
                    size = lax.rsqrt(jnp.mean(o * o, axis=1, keepdims=True) + norm_eps)
                    normed[rows, k * DK : (k + 1) * DK] = (o * size * out_gain[...]).astype(bf16)
                if d:
                    mixer.there(r, d).start()
        mixer.run(gather.finish)


def layer_pass(doc, tokens, gain, wk, wv, wb, wq, out_gain, wo):
    length, width = tokens.shape
    heads = wb.shape[0]
    tiles = length // TILE
    depth = wo.shape[0]
    chips = wo.shape[1] // depth // 2
    part = length // chips
    sub = part // SUBS
    message = (heads * DK + 16, 2 * DK)
    dma = lambda *shape: pltpu.SemaphoreType.DMA(shape)
    whole = lambda shape: pl.BlockSpec(
        shape, lambda i, doc: (0,) * len(shape), pipeline_mode=pl.Buffered(1)
    )
    return pl.pallas_call(
        layer_kernel,
        grid_spec=pltpu.PrefetchScalarGridSpec(
            num_scalar_prefetch=1,
            grid=(2 * tiles + 1,),
            in_specs=[
                pl.BlockSpec(
                    (TILE, width),
                    lambda i, doc: (
                        jnp.where(i > tiles, i - tiles - 1, jnp.minimum(i, tiles - 1)),
                        0,
                    ),
                ),
                whole((1, width)),
                whole(wk.shape),
                whole(wv.shape),
                whole(wb.shape),
                whole(wq.shape),
                whole(out_gain.shape),
                pl.BlockSpec(memory_space=pl.ANY),
            ],
            out_specs=pl.BlockSpec(memory_space=pl.ANY),
            scratch_shapes=[
                pltpu.VMEM((width, 5 * DK), bf16),
                pltpu.VMEM(wq.shape, bf16),
                pltpu.VMEM((heads, length, DK), bf16),
                pltpu.VMEM((2, heads, TILE, DK), f32),
                pltpu.VMEM((2, TILE, DK), f32),
                pltpu.VMEM((length, DK), f32),
                pltpu.VMEM((heads, length, 2 * DK), bf16),
                pltpu.VMEM((heads, length // DK, DK, 2 * DK), bf16),
                pltpu.VMEM((heads, DK, 2 * DK), f32),
                pltpu.VMEM((STEP, STEP), f32),
                pltpu.VMEM((STEP, STEP), f32),
                pltpu.VMEM((2, STEP, STEP), bf16),
                pltpu.VMEM((len(LEVELS), STEP, STEP), bf16),
                pltpu.VMEM((heads, length, DK), f32),
                pltpu.VMEM((heads, length, DK), bf16),
                pltpu.VMEM(message, bf16),
                pltpu.VMEM((2,) + message, bf16),
                pltpu.VMEM(message, bf16),
                pltpu.VMEM(message, bf16),
                pltpu.VMEM((message[0], DK), bf16),
                pltpu.VMEM((length, heads * DK), bf16),
                pltpu.VMEM((part, wo.shape[1]), bf16),
                pltpu.VMEM((2 * chips, depth, wo.shape[1] // 2), bf16),
                pltpu.VMEM((SUBS, chips, sub, depth), bf16),
                dma(chips - 1, 2, 2),
                dma(chips - 1, 2, 2),
                dma(3),
                dma(2, SIDE - 1),
                dma(2, SIDE - 1),
                dma(4),
                dma(4),
            ]
            + [dma(SUBS, chips)] * 6,
        ),
        out_shape=jax.ShapeDtypeStruct((length, heads * DK), bf16),
        compiler_params=pltpu.CompilerParams(
            vmem_limit_bytes=58 << 20, collective_id=0, has_side_effects=True
        ),
        name="layer_pass",
    )(doc, tokens, gain, wk, wv, wb, wq, out_gain, wo)


def local(tokens, norm_gain, wq, wk, wv, wb, out_gain, wo, block_doc):
    return layer_pass(
        block_doc, tokens, norm_gain[None, :], wk, wv, wb.T, wq, out_gain[None, :], wo
    )


def solution(mesh):
    in_specs = (
        P("seq", None),
        P(),
        P(None, "head"),
        P(None, "head"),
        P(None, "head"),
        P(None, "head"),
        P(),
        P("head", None),
        P("seq"),
    )
    return jax.shard_map(
        local, mesh=mesh, in_specs=in_specs, out_specs=P("seq", "head"), check_vma=False
    )
```

```python
import jax
import jax.numpy as jnp
from jax import lax
from jax.experimental import pallas as pl
from jax.experimental.pallas import tpu as pltpu
from jax.sharding import PartitionSpec as P

norm_eps = 1e-05
key_eps = 1e-06
BLOCK = 64
DK = 128
STEP = 256
TILE = 512
SIDE = 4
SPREAD_AT = 2
RINGED = 1
SUBS = 4
f32 = jnp.float32
bf16 = jnp.bfloat16
LEVELS = (2, 4, 8, 16, 32, 64)


def dot(a, b):
    return jnp.dot(a, b, preferred_element_type=f32)


def dot_nt(a, b):
    return lax.dot_general(a, b, (((1,), (1,)), ((), ())), preferred_element_type=f32)


def dot_tn(a, b):
    return lax.dot_general(a, b, (((0,), (0,)), ((), ())), preferred_element_type=f32)


def unit(values):
    act = values * jax.nn.sigmoid(values)
    return act * lax.rsqrt(jnp.sum(act * act, axis=1, keepdims=True) + key_eps)


def peer(s, h):
    return dict(device_id=(s, h), device_id_type=pl.DeviceIdType.MESH)


def fill_masks(strict, causal, pair, off):
    shape = (STEP, STEP)
    row = lax.broadcasted_iota(jnp.int32, shape, 0)
    col = lax.broadcasted_iota(jnp.int32, shape, 1)
    same = (row // DK) == (col // DK)
    strict[...] = jnp.where(same & (row > col), 1.0, 0.0).astype(f32)
    causal[...] = jnp.where(same & (row >= col), 1.0, 0.0).astype(f32)
    pair[0] = jnp.where((row // 2 == col // 2) & (row > col), 1.0, 0.0).astype(bf16)
    pair[1] = jnp.where(row == col, 1.0, 0.0).astype(bf16)
    for n, s in enumerate(LEVELS):
        hit = (row // (2 * s) == col // (2 * s)) & (row // s > col // s)
        off[n] = jnp.where(hit, 1.0, 0.0).astype(bf16)


def scaled_weight(weight, gain):
    column = jnp.transpose(jnp.broadcast_to(gain[...], (DK, gain.shape[1])))
    parts = [
        weight[:, n * DK : (n + 1) * DK].astype(f32) * column for n in range(weight.shape[1] // DK)
    ]
    return jnp.concatenate(parts, axis=1).astype(bf16)


def doc_masks(doc, at):
    d = [doc[at + j] for j in range(4)]
    before = doc[jnp.maximum(at - 1, 0)]
    link = [
        jnp.where((before == d[0]) | (at == 0), 1.0, 0.0).astype(f32),
        jnp.where(d[1] == d[2], 1.0, 0.0).astype(f32),
    ]
    join = [
        jnp.where(d[0] == d[1], 1.0, 0.0).astype(f32),
        jnp.where(d[2] == d[3], 1.0, 0.0).astype(f32),
    ]
    row = lax.broadcasted_iota(jnp.int32, (STEP, 1), 0)
    second = (row % DK) >= BLOCK
    join_r = jnp.where(row >= DK, join[1], join[0])
    link_r = jnp.where(row >= DK, link[1], link[0])
    enters = jnp.where(second, link_r * join_r, link_r)
    leaves = jnp.where(second, 1.0, join_r)
    cross = jnp.where(second, join_r, 1.0)
    col = lax.broadcasted_iota(jnp.int32, (1, STEP), 1)
    full = jnp.where((col % DK) < BLOCK, cross, 1.0)
    return enters, leaves, full, [link[c] * join[c] for c in range(2)]


def upper(a, size):
    return jnp.concatenate([a[j : j + size] for j in range(0, a.shape[0], 2 * size)], axis=0)


def lower(a, size):
    return jnp.concatenate([a[j + size : j + 2 * size] for j in range(0, a.shape[0], 2 * size)], axis=0)


def spread_rows(first, second, size):
    parts = []
    for j in range(0, first.shape[0], size):
        parts += [first[j : j + size], second[j : j + size]]
    return jnp.concatenate(parts, axis=0)


def interleave(main, side, every):
    count = 0
    for _ in main:
        count += 1
        if count % every == 0:
            next(side, None)
    for _ in side:
        pass


def project_keys(x, scale_out, weights, keys_at, vbuf, bbuf, slot):
    halves = x.shape[0] // STEP
    scales = []
    for m in range(halves):
        rows = slice(m * STEP, (m + 1) * STEP)
        floats = x[rows, :].astype(f32)
        r = lax.rsqrt(jnp.mean(floats * floats, axis=1, keepdims=True) + norm_eps)
        scales.append(r)
        scale_out[rows, :] = jnp.broadcast_to(r, (STEP, DK))
        yield
        b = dot(x[rows, :], weights[:, 4 * DK :]) * r
        bbuf[slot, rows, :] = jax.nn.sigmoid(b)
        yield
        for h in range(2):
            kv = dot(x[rows, :], weights[:, 2 * h * DK : 2 * (h + 1) * DK]) * r
            keys_at[h, rows, :] = unit(kv[:, :DK]).astype(bf16)
            vbuf[slot, h, rows, :] = kv[:, DK:]
            yield


def solve_keys(doc, at, keys_at, vbuf, bbuf, slot, ps, masks, wu_out, ps_all):
    strict, pair, off = masks
    halves = keys_at.shape[1] // STEP
    groups = [(h, g) for g in range(halves) for h in range(2)]
    dm = [doc_masks(doc, at + 4 * g) for g in range(halves)]
    keys, a_hi, a_lo, xb, t, right, y, wu = {}, {}, {}, {}, {}, {}, {}, {}
    beta = {}
    for h, g in groups:
        rows = slice(g * STEP, (g + 1) * STEP)
        keys[h, g] = keys_at[h, rows, :]
        beta[h, g] = bbuf[slot, rows, h : h + 1]
        a = dot_nt(keys[h, g], keys[h, g]) * beta[h, g] * (strict[...] * dm[g][2])
        hi = a.astype(bf16)
        a_hi[h, g] = hi
        a_lo[h, g] = (a - hi.astype(f32)).astype(bf16)
        xb[h, g] = pair[1] - hi * pair[0]
        yield
    for n, size in enumerate(LEVELS):
        if size < 16:
            for k in groups:
                t[k] = dot(a_hi[k] * off[n], xb[k]).astype(bf16)
            yield
            for k in groups:
                xb[k] = xb[k] - dot(xb[k], t[k]).astype(bf16)
            yield
            continue
        for k in groups:
            low = dot(lower(a_hi[k], size) * lower(off[n], size), xb[k]).astype(bf16)
            t[k] = spread_rows(jnp.zeros_like(low), low, size)
        yield
        for k in groups:
            low = lower(xb[k], size)
            low = low - dot(low, t[k]).astype(bf16)
            xb[k] = spread_rows(upper(xb[k], size), low, size)
        yield
    for h, g in groups:
        rows = slice(g * STEP, (g + 1) * STEP)
        b = beta[h, g]
        right[h, g] = jnp.concatenate(
            [(b * dm[g][0]) * keys[h, g].astype(f32), b * vbuf[slot, h, rows, :]], axis=1
        )
        y[h, g] = dot(xb[h, g], right[h, g].astype(bf16)).astype(bf16)
    yield
    left = {}
    for k in groups:
        rest = right[k] - y[k].astype(f32) - dot(a_hi[k], y[k]) - dot(a_lo[k], y[k])
        left[k] = rest.astype(bf16)
    yield
    for h, g in groups:
        wu[h, g] = (y[h, g].astype(f32) + dot(xb[h, g], left[h, g])).astype(bf16)
        wu_out[h, g * STEP : (g + 1) * STEP, :] = wu[h, g]
    yield
    step = {}
    for h, g in groups:
        k_end = (keys[h, g].astype(f32) * dm[g][1]).astype(bf16)
        for c in range(2):
            rows = slice(c * DK, (c + 1) * DK)
            step[h, g, c] = dot_tn(k_end[rows], wu[h, g][rows])
    yield
    for g in range(halves):
        for c in range(2):
            for h in range(2):
                state = ps[h]
                sb = state.astype(bf16)
                ps_all[h, 2 * g + c] = sb
                move = step[h, g, c]
                moved = dot(move[:, :DK].astype(bf16), sb)
                gain = jnp.concatenate([jnp.zeros((DK, DK), f32), move[:, DK:]], axis=1)
                ps[h] = dm[g][3][c] * state - moved + gain
            yield


def query_tile(doc, at, x, scale, weights, keys, wu, ps_all, causal, out, carried):
    groups = [(h, g) for g in range(x.shape[0] // STEP) for h in range(2)]
    dm = [doc_masks(doc, at + 4 * g) for g in range(x.shape[0] // STEP)]
    qb, mixed, scores = {}, {}, {}
    for g in range(x.shape[0] // STEP):
        rows = slice(g * STEP, (g + 1) * STEP)
        both = dot(x[rows, :], weights[...]) * scale[rows, 0:1]
        for h in range(2):
            qb[h, g] = unit(both[:, h * DK : (h + 1) * DK]).astype(bf16)
    for h, g in groups:
        rows = slice(g * STEP, (g + 1) * STEP)
        s = dot_nt(qb[h, g], keys[h, rows, :]) * (causal[...] * dm[g][2])
        scores[h, g] = s.astype(bf16)
    for h, g in groups:
        rows = slice(g * STEP, (g + 1) * STEP)
        mixed[h, g] = dot(scores[h, g], wu[h, rows, :])
    for h, g in groups:
        reach = (dm[g][0] * qb[h, g].astype(f32) - mixed[h, g][:, :DK]).astype(bf16)
        for c in range(2):
            rows = slice(c * DK, (c + 1) * DK)
            to = slice(g * STEP + c * DK, g * STEP + (c + 1) * DK)
            seen = dot(reach[rows], ps_all[h, 2 * g + c])
            carried[h, to, :] = seen[:, :DK].astype(bf16)
            out[h, to, :] = mixed[h, g][rows, DK:] + seen[:, DK:]


class Place:
    def __init__(self):
        self.s, h = lax.axis_index("seq"), lax.axis_index("head")
        self.length = lax.axis_size("seq")
        self.chips = lax.axis_size("head") // 2
        self.y, self.c = h // 2, lax.rem(h, 2)
        self.outer, self.inner = self.s // SIDE, lax.rem(self.s, SIDE)

    def later(self, d):
        return peer(lax.rem(self.s + d + self.length, self.length), self.y * 2 + self.c)

    def chip(self, d, core):
        return peer(self.s, lax.rem(self.y + d + self.chips, self.chips) * 2 + core)

    def beside(self):
        return self.chip(0, 1 - self.c)

    def along(self, axis, d):
        if axis == 0:
            s = lax.rem(self.outer + d + SIDE, SIDE) * SIDE + self.inner
        else:
            s = self.outer * SIDE + lax.rem(self.inner + d + SIDE, SIDE)
        return peer(s, self.y * 2 + self.c)

    def peers(self):
        found = [self.chip(d, core) for d in range(1, self.chips) for core in range(2)]
        found.append(self.beside())
        found += [self.along(a, d) for a in range(2) for d in range(1, SIDE)]
        return found + [self.later(d) for d in (1, -1, 2, -2, 4, -4)]


class WeightGather:
    def __init__(self, me, wo, w, over_s, over_r, near_s, ring_s, ring_r):
        self.me, self.wo, self.w = me, wo, w
        self.over_s, self.over_r, self.near_s = over_s, over_r, near_s
        self.ring_s, self.ring_r = ring_s, ring_r
        self.depth, self.half = w.shape[1], w.shape[2]
        self.quarter, self.wide = self.depth // SIDE, self.half // 2

    def rows(self, axis):
        q = self.me.outer if axis == 0 else self.me.inner
        return pl.ds(pl.multiple_of(q * self.quarter, self.quarter), self.quarter)

    def over(self, d, core, axis, origin):
        start = core * self.half + axis * self.wide
        block = (self.me.chips - d) * 2 + origin
        rows = self.rows(axis) if axis < RINGED else slice(None)
        return pltpu.make_async_remote_copy(
            src_ref=self.wo.at[rows, start : start + self.wide],
            dst_ref=self.w.at[block, rows, axis * self.wide : (axis + 1) * self.wide],
            send_sem=self.over_s.at[d - 1, core, axis],
            recv_sem=self.over_r.at[d - 1, origin, axis],
            **self.me.chip(d, core),
        )

    def columns(self, core):
        return pl.ds(pl.multiple_of(core * self.half, self.half), self.half)

    def pair(self):
        return pltpu.make_async_remote_copy(
            src_ref=self.wo.at[:, self.columns(1 - self.me.c)],
            dst_ref=self.w.at[self.me.c],
            send_sem=self.near_s.at[0],
            recv_sem=self.near_s.at[1],
            **self.me.beside(),
        )

    def own(self):
        return pltpu.make_async_copy(
            self.wo.at[:, self.columns(self.me.c)], self.w.at[self.me.c], self.near_s.at[2]
        )

    def ring(self, axis, d):
        at = self.w.at[2:, self.rows(axis), axis * self.wide : (axis + 1) * self.wide]
        return pltpu.make_async_remote_copy(
            src_ref=at,
            dst_ref=at,
            send_sem=self.ring_s.at[axis, d - 1],
            recv_sem=self.ring_r.at[axis, d - 1],
            **self.me.along(axis, d),
        )

    def each_over(self):
        return [(d, k, a) for a in range(2) for d in (2, 1, 3) for k in range(2)]

    def each_ring(self):
        return [(a, d) for d in (2, 1, 3) for a in range(RINGED)]

    def begin(self):
        for d, core, axis in self.each_over():
            self.over(d, core, axis, self.me.c).start()
        self.pair().start()
        self.own().start()

    def spread(self):
        for d, core, axis in self.each_over():
            if axis < RINGED:
                self.over(d, core, axis, core).wait_recv()
        for at in self.each_ring():
            self.ring(*at).start()

    def finish(self):
        for d, core, axis in self.each_over():
            self.over(d, core, axis, self.me.c).wait_send()
            if axis >= RINGED:
                self.over(d, core, axis, core).wait_recv()
        self.pair().wait()
        self.own().wait()
        for at in self.each_ring():
            self.ring(*at).wait()


def join(first, then, follows):
    moved = jnp.where(follows, dot(then[:, :DK], first), 0.0)
    gain = jnp.concatenate([jnp.zeros((DK, DK), f32), then[:, DK:].astype(f32)], axis=1)
    return (moved + gain).astype(bf16)


class StateExchange:
    def __init__(self, me, own, near, three, far1, far4, send, recv):
        self.me = me
        self.own, self.near, self.three, self.far1, self.far4 = own, near, three, far1, far4
        self.send, self.recv = send, recv
        self.foot = own.shape[0] - 16

    def move(self, src, dst, at, d):
        return pltpu.make_async_remote_copy(
            src_ref=src, dst_ref=dst, send_sem=self.send.at[at], recv_sem=self.recv.at[at],
            **self.me.later(d),
        )

    def first_round(self):
        return [self.move(self.own, self.near.at[1], 1, 2), self.move(self.own, self.near.at[0], 0, 1)]

    def second_round(self):
        return [
            self.move(self.three, self.far1, 2, 1),
            self.move(self.three.at[:, DK:], self.far4, 3, 4),
        ]

    def begin(self, ps, first_doc, last_doc):
        foot = self.foot
        for k in range(ps.shape[0]):
            self.own[k * DK : (k + 1) * DK, :] = ps[k].astype(bf16)
        self.own[foot:, :DK] = jnp.full((16, DK), first_doc.astype(f32)).astype(bf16)
        self.own[foot:, DK:] = jnp.full((16, DK), last_doc.astype(f32)).astype(bf16)
        for copy in self.first_round():
            copy.start()

    def again(self):
        for copy in self.first_round():
            copy.wait()
        foot, own, near, s = self.foot, self.own, self.near, self.me.s
        first_own, last_one = own[foot : foot + 1, 0:1], near[0, foot : foot + 1, DK : DK + 1]
        first_one, last_two = near[0, foot : foot + 1, 0:1], near[1, foot : foot + 1, DK : DK + 1]
        for k in range(foot // DK):
            rows = slice(k * DK, (k + 1) * DK)
            two = join(near[1, rows, :], near[0, rows, :], (last_two == first_one) & (s >= 2))
            self.three[rows, :] = join(two, own[rows, :], (last_one == first_own) & (s >= 1))
        self.three[foot:, :DK] = near[1, foot:, :DK]
        self.three[foot:, DK:] = own[foot:, DK:]
        for copy in self.second_round():
            copy.start()

    def entering(self):
        for copy in self.second_round():
            copy.wait()
        foot, far1, far4, s = self.foot, self.far1, self.far4, self.me.s
        first_own, last_one = self.own[foot : foot + 1, 0:1], far1[foot : foot + 1, DK : DK + 1]
        first_three, last_four = far1[foot : foot + 1, 0:1], far4[foot : foot + 1, 0:1]
        states = []
        for k in range(foot // DK):
            rows = slice(k * DK, (k + 1) * DK)
            older = jnp.where(
                (last_four == first_three) & (s >= 4), dot(far1[rows, :DK], far4[rows, :]), 0.0
            )
            state = older + far1[rows, DK:].astype(f32)
            states.append(jnp.where((last_one == first_own) & (s >= 1), state, 0.0).astype(bf16))
        return states


class Mixer:
    def __init__(self, me, normed, gath, w, obuf, result, there_s, there_r, share_s, share_r, back_s, back_r):
        self.me, self.normed, self.gath, self.w = me, normed, gath, w
        self.obuf, self.result = obuf, result
        self.there_s, self.there_r, self.share_s, self.share_r = there_s, there_r, share_s, share_r
        self.back_s, self.back_r = back_s, back_r
        self.width = normed.shape[1]
        self.part = normed.shape[0] // me.chips
        self.sub = self.part // SUBS

    def rows(self, d, r):
        chip_at = lax.rem(self.me.y + d + self.me.chips, self.me.chips)
        return pl.ds(pl.multiple_of(chip_at * self.part + r * self.sub, self.sub), self.sub)

    def spot(self, r, d, core):
        block = (self.me.chips - d) % self.me.chips * 2 + core
        lanes = pl.ds(pl.multiple_of(block * self.width, self.width), self.width)
        return self.gath.at[r * self.sub : (r + 1) * self.sub, lanes]

    def there(self, r, d):
        return pltpu.make_async_remote_copy(
            src_ref=self.normed.at[self.rows(d, r), :],
            dst_ref=self.spot(r, d, self.me.c),
            send_sem=self.there_s.at[r, d],
            recv_sem=self.there_r.at[r, d],
            **self.me.chip(d, self.me.c),
        )

    def share(self, r, d):
        at = self.spot(r, d, self.me.c)
        return pltpu.make_async_remote_copy(
            src_ref=self.normed.at[self.rows(0, r), :] if d == 0 else at,
            dst_ref=at,
            send_sem=self.share_s.at[r, d],
            recv_sem=self.share_r.at[r, d],
            **self.me.beside(),
        )

    def back(self, r, t, e):
        return pltpu.make_async_remote_copy(
            src_ref=self.obuf.at[r, t],
            dst_ref=self.result.at[self.rows(0, r), :],
            send_sem=self.back_s.at[r, t],
            recv_sem=self.back_r.at[r, e],
            **peer(self.me.s, 2 * self.me.chips // 2 * self.me.c + t),
        )

    def home(self, r, t):
        return pltpu.make_async_copy(
            self.obuf.at[r, t], self.result.at[self.rows(0, r), :], self.back_s.at[r, t]
        )

    def target(self, t):
        at = self.me.chips * self.me.c + t
        far = lax.rem(at // 2 - self.me.y + self.me.chips, self.me.chips)
        return far, at == self.me.y * 2 + self.me.c

    def run(self, weight_here):
        me, chips = self.me, self.me.chips
        order = [2, 1, 3]
        for r in range(SUBS):
            self.share(r, 0).start()
            self.spot(r, 0, me.c)[...] = self.normed[self.rows(0, r), :]
        for r in range(SUBS):
            for d in [1, 3, 2]:
                self.there(r, d).wait_recv()
                self.share(r, d).start()
            for d in range(chips):
                self.share(r, d).wait_recv()
            if r == 0:
                weight_here()
            block = self.gath[r * self.sub : (r + 1) * self.sub, :]
            w = self.w[...].reshape(self.w.shape[0] * self.w.shape[1], self.w.shape[2])
            for t in range(chips):
                cut = w[:, t * self.width : (t + 1) * self.width]
                self.obuf[r, t] = dot(block, cut).astype(bf16)
                far, mine = self.target(t)

                @pl.when(jnp.logical_not(mine))
                def _():
                    self.back(r, t, far).start()

                @pl.when(mine)
                def _():
                    self.home(r, t).start()

        for r in range(SUBS):
            for d in order:
                self.there(r, d).wait_send()
            for d in range(chips):
                self.share(r, d).wait_send()
            for t in range(chips):
                far, mine = self.target(t)

                @pl.when(jnp.logical_not(mine))
                def _():
                    self.back(r, t, far).wait_send()

                @pl.when(mine)
                def _():
                    self.home(r, t).wait()

            for e in range(1, chips):
                self.back(r, 0, e).wait_recv()

            @pl.when(me.c != me.y // (chips // 2))
            def _():
                self.back(r, 0, 0).wait_recv()


def layer_kernel(
    doc, x, gain, wk, wv, wb, wq, out_gain, wo, result,
    weights, wqs, keys, vbuf, bbuf, scale, wu, ps_all, ps, strict, causal, pair, off,
    out, carried, own, near, three, far1, far4, normed, gath, w, obuf,
    over_s, over_r, near_s, ring_s, ring_r, st_s, st_r,
    there_s, there_r, share_s, share_r, back_s, back_r,
):
    i = pl.program_id(0)
    tile, count = x.shape[0], doc.shape[0]
    blocks = tile // BLOCK
    tiles = count // blocks
    me = Place()
    gather = WeightGather(me, wo, w, over_s, over_r, near_s, ring_s, ring_r)
    states = StateExchange(me, own, near, three, far1, far4, st_s, st_r)
    mixer = Mixer(
        me, normed, gath, w, obuf, result, there_s, there_r, share_s, share_r, back_s, back_r
    )

    def at_tile(j):
        return pl.ds(pl.multiple_of(j * tile, tile), tile)

    def project():
        at = at_tile(jnp.minimum(i, tiles - 1))
        return project_keys(x, scale.at[at, :], weights, keys.at[:, at, :], vbuf, bbuf, i % 2)

    def solve():
        j = jnp.clip(i - 1, 0, tiles - 1)
        at = at_tile(j)
        chunks = pl.ds(pl.multiple_of(j * (tile // DK), tile // DK), tile // DK)
        return solve_keys(
            doc, j * blocks, keys.at[:, at, :], vbuf, bbuf, (i + 1) % 2, ps,
            (strict, pair, off), wu.at[:, at, :], ps_all.at[:, chunks],
        )

    @pl.when(i == 0)
    def _():
        barrier = pltpu.get_barrier_semaphore()
        for at in me.peers():
            pl.semaphore_signal(barrier, inc=1, **at)
        fill_masks(strict, causal, pair, off)
        sk, sv = scaled_weight(wk, gain), scaled_weight(wv, gain)
        for h in range(2):
            weights[:, 2 * h * DK : (2 * h + 1) * DK] = sk[:, h * DK : (h + 1) * DK]
            weights[:, (2 * h + 1) * DK : (2 * h + 2) * DK] = sv[:, h * DK : (h + 1) * DK]
        rest = jnp.zeros((DK - wb.shape[0], wb.shape[1]), f32)
        padded = jnp.concatenate([wb[...].astype(f32) * gain[...], rest], axis=0)
        weights[:, 4 * DK :] = jnp.transpose(padded).astype(bf16)
        pl.semaphore_wait(barrier, len(me.peers()))
        gather.begin()
        row = lax.broadcasted_iota(jnp.int32, (DK, 2 * DK), 0)
        col = lax.broadcasted_iota(jnp.int32, (DK, 2 * DK), 1)
        for h in range(2):
            ps[h] = jnp.where(row == col, 1.0, 0.0).astype(f32)
        for _ in project():
            pass

    @pl.when(i == SPREAD_AT)
    def _():
        gather.spread()

    @pl.when((i > 0) & (i < tiles))
    def _():
        interleave(solve(), project(), 2)

    @pl.when(i == tiles)
    def _():
        for _ in solve():
            pass
        states.begin(ps, doc[0], doc[count - 1])
        wqs[...] = scaled_weight(wq, gain)

    @pl.when(i == 2 * tiles)
    def _():
        states.again()

    @pl.when(i > tiles)
    def _():
        j = jnp.clip(i - tiles - 1, 0, tiles - 1)
        at = at_tile(j)
        chunks = pl.ds(pl.multiple_of(j * (tile // DK), tile // DK), tile // DK)
        query_tile(
            doc, j * blocks, x, scale.at[at, :], wqs, keys.at[:, at, :], wu.at[:, at, :],
            ps_all.at[:, chunks], causal, out.at[:, at, :], carried.at[:, at, :],
        )

    @pl.when(i == 2 * tiles)
    def _():
        entering = states.entering()
        turns = [(r, d) for r in range(SUBS) for d in (2, 1, 3)]
        for r, d in turns + [(r, 0) for r in range(SUBS)]:
                rows = mixer.rows(d, r)
                for k in range(len(entering)):
                    o = out[k, rows, :] + dot(carried[k, rows, :], entering[k])
                    size = lax.rsqrt(jnp.mean(o * o, axis=1, keepdims=True) + norm_eps)
                    normed[rows, k * DK : (k + 1) * DK] = (o * size * out_gain[...]).astype(bf16)
                if d:
                    mixer.there(r, d).start()
        mixer.run(gather.finish)


def layer_pass(doc, tokens, gain, wk, wv, wb, wq, out_gain, wo):
    length, width = tokens.shape
    heads = wb.shape[0]
    tiles = length // TILE
    depth = wo.shape[0]
    chips = wo.shape[1] // depth // 2
    part = length // chips
    sub = part // SUBS
    message = (heads * DK + 16, 2 * DK)
    dma = lambda *shape: pltpu.SemaphoreType.DMA(shape)
    whole = lambda shape: pl.BlockSpec(
        shape, lambda i, doc: (0,) * len(shape), pipeline_mode=pl.Buffered(1)
    )
    return pl.pallas_call(
        layer_kernel,
        grid_spec=pltpu.PrefetchScalarGridSpec(
            num_scalar_prefetch=1,
            grid=(2 * tiles + 1,),
            in_specs=[
                pl.BlockSpec(
                    (TILE, width),
                    lambda i, doc: (
                        jnp.where(i > tiles, i - tiles - 1, jnp.minimum(i, tiles - 1)),
                        0,
                    ),
                ),
                whole((1, width)),
                whole(wk.shape),
                whole(wv.shape),
                whole(wb.shape),
                whole(wq.shape),
                whole(out_gain.shape),
                pl.BlockSpec(memory_space=pl.ANY),
            ],
            out_specs=pl.BlockSpec(memory_space=pl.ANY),
            scratch_shapes=[
                pltpu.VMEM((width, 5 * DK), bf16),
                pltpu.VMEM(wq.shape, bf16),
                pltpu.VMEM((heads, length, DK), bf16),
                pltpu.VMEM((2, heads, TILE, DK), f32),
                pltpu.VMEM((2, TILE, DK), f32),
                pltpu.VMEM((length, DK), f32),
                pltpu.VMEM((heads, length, 2 * DK), bf16),
                pltpu.VMEM((heads, length // DK, DK, 2 * DK), bf16),
                pltpu.VMEM((heads, DK, 2 * DK), f32),
                pltpu.VMEM((STEP, STEP), f32),
                pltpu.VMEM((STEP, STEP), f32),
                pltpu.VMEM((2, STEP, STEP), bf16),
                pltpu.VMEM((len(LEVELS), STEP, STEP), bf16),
                pltpu.VMEM((heads, length, DK), f32),
                pltpu.VMEM((heads, length, DK), bf16),
                pltpu.VMEM(message, bf16),
                pltpu.VMEM((2,) + message, bf16),
                pltpu.VMEM(message, bf16),
                pltpu.VMEM(message, bf16),
                pltpu.VMEM((message[0], DK), bf16),
                pltpu.VMEM((length, heads * DK), bf16),
                pltpu.VMEM((part, wo.shape[1]), bf16),
                pltpu.VMEM((2 * chips, depth, wo.shape[1] // 2), bf16),
                pltpu.VMEM((SUBS, chips, sub, depth), bf16),
                dma(chips - 1, 2, 2),
                dma(chips - 1, 2, 2),
                dma(3),
                dma(2, SIDE - 1),
                dma(2, SIDE - 1),
                dma(4),
                dma(4),
            ]
            + [dma(SUBS, chips)] * 6,
        ),
        out_shape=jax.ShapeDtypeStruct((length, heads * DK), bf16),
        compiler_params=pltpu.CompilerParams(
            vmem_limit_bytes=58 << 20, collective_id=0, has_side_effects=True
        ),
        name="layer_pass",
    )(doc, tokens, gain, wk, wv, wb, wq, out_gain, wo)


def local(tokens, norm_gain, wq, wk, wv, wb, out_gain, wo, block_doc):
    return layer_pass(
        block_doc, tokens, norm_gain[None, :], wk, wv, wb.T, wq, out_gain[None, :], wo
    )


def solution(mesh):
    in_specs = (
        P("seq", None),
        P(),
        P(None, "head"),
        P(None, "head"),
        P(None, "head"),
        P(None, "head"),
        P(),
        P("head", None),
        P("seq"),
    )
    return jax.shard_map(
        local, mesh=mesh, in_specs=in_specs, out_specs=P("seq", "head"), check_vma=False
    )
```
